256 devices in a mesh: gx: 32 (over z, x), gy: 8 (over y, core).
Axes of the slice: x: 4, y: 4, z: 8, core: 2. Of those that a mesh axis runs over, the one named last changes fastest.
Arguments:
- velocity: float32 [1, 2048, 2048], P(None, 'gx', 'gy'), may hold values from -6 to 6
Outputs:
- du_dx: float32 [1, 2048, 2048], P(None, 'gx', 'gy')
- du_dy: float32 [1, 2048, 2048], P(None, 'gx', 'gy')
- d2u_dx2: float32 [1, 2048, 2048], P(None, 'gx', 'gy')
- d2u_dy2: float32 [1, 2048, 2048], P(None, 'gx', 'gy')
The draws below stay inside these ranges and needn't reach their ends.
All inputs are finite; a program needn't handle non-finite values.
Results may differ from the reference program's by a relative error of at most 0.00007.
Values sent between devices are 32-bit elements; how exact they have to be, the bound alone decides.
A program may use at most 64 MiB of HBM per device.

```python
import jax
import jax.numpy as jnp
from jax import lax

NX = 2048
NY = 2048
PLANES = 1


def steps_of(key, dims, split, smallest, largest):
    loudness = 1.0
    for axis_at, blocks in split:
        heights = jax.random.uniform(jax.random.fold_in(jax.random.fold_in(key, 6), axis_at), (blocks,), jnp.float32, smallest / len(split), largest / len(split))
        loudness = loudness * jnp.repeat(jnp.exp(heights), dims[axis_at] // blocks).reshape((-1,) + (1,) * (len(dims) - 1 - axis_at))
    return loudness


def noise(own_key, extent, width, bound, shards=(), kind=jnp.bfloat16):
    entries = jax.random.normal(own_key, extent, jnp.float32) * width
    if len(shards) > 0:
        entries = steps_of(own_key, extent, shards, -0.22, 0.18) * entries
    return jnp.clip(entries, min=-bound, max=bound).astype(kind)


def setup_inputs(seed: int = 0) -> dict:
    key_of = jax.random.split(jax.random.key(seed), 2)
    velocity = noise(key_of[0], (PLANES, NX, NY), 1.0, 6.0, ((1, 32), (2, 8)), jnp.float32)
    return {"velocity": velocity}


FIRST_NEAR = 7.0 / 9.0
FIRST_FAR = 1.0 / 36.0
SECOND_NEAR = 12.0 / 11.0
SECOND_FAR = 3.0 / 44.0
FIRST_COUPLING = 1.0 / 3.0
SECOND_COUPLING = 2.0 / 11.0


def stencils(field, axis):
    plus_one = jnp.roll(field, -1, axis)
    minus_one = jnp.roll(field, 1, axis)
    plus_two = jnp.roll(field, -2, axis)
    minus_two = jnp.roll(field, 2, axis)
    first_order = FIRST_NEAR * (plus_one - minus_one) + FIRST_FAR * (plus_two - minus_two)
    second_order = SECOND_NEAR * (plus_one - 2.0 * field + minus_one) + SECOND_FAR * (plus_two - 2.0 * field + minus_two)
    return first_order, second_order


def periodic_solve(source, coupling, axis):
    length = source.shape[axis]
    waves = jnp.arange(length).astype(source.dtype) * (2.0 * jnp.pi / length)
    divisor = 1.0 + 2.0 * coupling * jnp.cos(waves)
    if axis == 0:
        divisor = divisor[:, None]
    else:
        divisor = divisor[None, :]
    spectrum = jnp.fft.fft(source, axis=axis) / divisor
    return jnp.real(jnp.fft.ifft(spectrum, axis=axis)).astype(source.dtype)


def one_plane(plane):
    first_x, second_x = stencils(plane, 0)
    first_y, second_y = stencils(plane, 1)
    return (periodic_solve(first_x, FIRST_COUPLING, 0), periodic_solve(first_y, FIRST_COUPLING, 1),
            periodic_solve(second_x, SECOND_COUPLING, 0), periodic_solve(second_y, SECOND_COUPLING, 1))


def reference(velocity):
    du_dx, du_dy, d2u_dx2, d2u_dy2 = lax.map(one_plane, velocity)
    return (du_dx, du_dy, d2u_dx2, d2u_dy2)
```

```python
import functools
import math

import jax
import jax.numpy as jnp
from jax import lax
from jax.experimental import pallas as pl
from jax.experimental.pallas import tpu as pltpu
from jax.sharding import PartitionSpec as P

FIRST_NEAR = 7.0 / 9.0
FIRST_FAR = 1.0 / 36.0
SECOND_NEAR = 12.0 / 11.0
SECOND_FAR = 3.0 / 44.0
COUPLINGS = (1.0 / 3.0, 2.0 / 11.0)
MESH = pl.DeviceIdType.MESH
HALO = 24
F32 = jnp.float32
BF16 = jnp.bfloat16


def green(coupling):
    root = math.sqrt(1.0 - 4.0 * coupling * coupling)
    return (1.0 - root) / (2.0 * coupling), 1.0 / root


def powers(coupling, distance):
    ratio, scale = green(coupling)
    size = scale * jnp.exp(distance.astype(F32) * math.log(ratio))
    return jnp.where(distance % 2 == 0, size, -size)


def stencils(u, axis):
    n = u.shape[axis]
    plus_one = pltpu.roll(u, n - 1, axis)
    minus_one = pltpu.roll(u, 1, axis)
    plus_two = pltpu.roll(u, n - 2, axis)
    minus_two = pltpu.roll(u, 2, axis)
    first = FIRST_NEAR * (plus_one - minus_one) + FIRST_FAR * (plus_two - minus_two)
    second = SECOND_NEAR * (plus_one - 2.0 * u + minus_one) + SECOND_FAR * (
        plus_two - 2.0 * u + minus_two
    )
    return first, second


def iota(shape, axis):
    return lax.broadcasted_iota(jnp.int32, shape, axis)


def split(a):
    high = a.astype(BF16)
    return high, (a - high.astype(F32)).astype(BF16)


def dot(a, b):
    return jnp.dot(a, b, preferred_element_type=F32)


def dot3(a, b):
    ah, al = split(a)
    bh, bl = split(b)
    return dot(ah, bh) + dot(al, bh) + dot(ah, bl)


def kernel(nx, ny, v_ref, dx_ref, dy_ref, dxx_ref, dyy_ref, u_ref, xl, xr, yl, yr, local_sem, send, recv):
    ix = lax.axis_index("gx")
    iy = lax.axis_index("gy")
    up = {"gx": lax.rem(ix + 1, nx)}
    down = {"gx": lax.rem(ix + nx - 1, nx)}
    right = {"gy": lax.rem(iy + 1, ny)}
    left = {"gy": lax.rem(iy + ny - 1, ny)}
    rows, cols = u_ref.shape

    load = pltpu.make_async_copy(v_ref.at[0], u_ref, local_sem)
    load.start()
    barrier = pltpu.get_barrier_semaphore()
    for other in (up, down, left, right):
        pl.semaphore_signal(barrier, inc=1, device_id=other, device_id_type=MESH)
    load.wait()
    pl.semaphore_wait(barrier, 4)

    copies = []
    for k, (src, dst, other) in enumerate(
        (
            (u_ref.at[pl.ds(rows - HALO, HALO), :], xl, up),
            (u_ref.at[pl.ds(0, HALO), :], xr, down),
            (u_ref.at[:, pl.ds(cols - 128, 128)], yl, right),
            (u_ref.at[:, pl.ds(0, 128)], yr, left),
        )
    ):
        copy = pltpu.make_async_remote_copy(
            src_ref=src,
            dst_ref=dst,
            send_sem=send.at[k],
            recv_sem=recv.at[k],
            device_id=other,
            device_id_type=MESH,
        )
        copy.start()
        copies.append(copy)

    u = u_ref[...]
    row = iota((rows, cols), 0)
    col = iota((rows, cols), 1)
    inner = (row >= 2) & (row < rows - 2)
    rx = [jnp.where(inner, s, 0.0) for s in stencils(u, 0)]
    distance = jnp.abs(iota((rows, rows), 0) - iota((rows, rows), 1))
    fx = [dot3(powers(c, distance), s) for c, s in zip(COUPLINGS, rx)]
    inner = (col >= 2) & (col < cols - 2)
    ry = [jnp.where(inner, s, 0.0) for s in stencils(u, 1)]
    distance = jnp.abs(iota((cols, cols), 0) - iota((cols, cols), 1))
    fy = [dot3(s, powers(c, distance)) for c, s in zip(COUPLINGS, ry)]

    for copy in copies:
        copy.wait_recv()

    edge = HALO + 8
    place = iota((edge, cols), 0)
    lower = stencils(jnp.concatenate([xl[...], u[:8]], axis=0), 0)
    upper = stencils(jnp.concatenate([u[rows - 8 :], xr[...]], axis=0), 0)
    for k, c in enumerate(COUPLINGS):
        _, scale = green(c)
        weight = jnp.where((place >= 2) & (place <= HALO), powers(c, jnp.abs(HALO - place)), 0.0)
        total = jnp.sum(weight * lower[k], axis=0, keepdims=True) / scale
        fx[k] += powers(c, row) * total + powers(c, jnp.abs(row - 1)) * lower[k][HALO + 1 : HALO + 2]
        weight = jnp.where((place >= 7) & (place < edge - 2), powers(c, jnp.abs(place - 7)), 0.0)
        total = jnp.sum(weight * upper[k], axis=0, keepdims=True) / scale
        fx[k] += (
            powers(c, rows - 1 - row) * total
            + powers(c, jnp.abs(rows - 2 - row)) * upper[k][6:7]
        )

    lane = iota((rows, 128), 1)
    lower = stencils(
        jnp.where(lane < 64, pltpu.roll(yl[...], 64, 1), pltpu.roll(u[:, :128], 64, 1)), 1
    )
    upper = stencils(
        jnp.where(lane < 64, pltpu.roll(u[:, cols - 128 :], 64, 1), pltpu.roll(yr[...], 64, 1)), 1
    )
    source = iota((128, 128), 0)
    target = iota((128, 128), 1)
    sides = [[], []]
    for k, c in enumerate(COUPLINGS):
        low = jnp.where((lane >= 2) & (lane < 66), lower[k], 0.0)
        sides[k].append(dot3(low, powers(c, jnp.abs(target - (source - 64)))))
        high = jnp.where((lane >= 62) & (lane < 126), upper[k], 0.0)
        sides[k].append(dot3(high, powers(c, jnp.abs(target - (source + 64)))))
        fy[k] += jnp.concatenate(sides[k], axis=1)

    dx_ref[0] = fx[0]
    dxx_ref[0] = fx[1]
    dy_ref[0] = fy[0]
    dyy_ref[0] = fy[1]
    for copy in copies:
        copy.wait_send()


def local(nx, ny, velocity):
    _, rows, cols = velocity.shape
    out = jax.ShapeDtypeStruct(velocity.shape, F32)
    return pl.pallas_call(
        functools.partial(kernel, nx, ny),
        out_shape=(out,) * 4,
        in_specs=[pl.BlockSpec(memory_space=pl.ANY)],
        out_specs=[pl.BlockSpec(memory_space=pltpu.VMEM)] * 4,
        scratch_shapes=[
            pltpu.VMEM((rows, cols), F32),
            pltpu.VMEM((HALO, cols), F32),
            pltpu.VMEM((HALO, cols), F32),
            pltpu.VMEM((rows, 128), F32),
            pltpu.VMEM((rows, 128), F32),
            pltpu.SemaphoreType.DMA,
            pltpu.SemaphoreType.DMA((4,)),
            pltpu.SemaphoreType.DMA((4,)),
        ],
        compiler_params=pltpu.CompilerParams(collective_id=0, has_side_effects=True),
    )(velocity)


def solution(mesh):
    placed = P(None, "gx", "gy")
    return jax.shard_map(
        functools.partial(local, mesh.shape["gx"], mesh.shape["gy"]),
        mesh=mesh,
        in_specs=(placed,),
        out_specs=(placed,) * 4,
        check_vma=False,
    )
```

```python
import functools
import math

import jax
import jax.numpy as jnp
from jax import lax
from jax.experimental import pallas as pl
from jax.experimental.pallas import tpu as pltpu
from jax.sharding import PartitionSpec as P

FIRST_NEAR = 7.0 / 9.0
FIRST_FAR = 1.0 / 36.0
SECOND_NEAR = 12.0 / 11.0
SECOND_FAR = 3.0 / 44.0
COUPLINGS = (1.0 / 3.0, 2.0 / 11.0)
MESH = pl.DeviceIdType.MESH
HALO = 24
F32 = jnp.float32
BF16 = jnp.bfloat16


def green(coupling):
    root = math.sqrt(1.0 - 4.0 * coupling * coupling)
    return (1.0 - root) / (2.0 * coupling), 1.0 / root


def powers(coupling, distance):
    ratio, scale = green(coupling)
    size = scale * jnp.exp(distance.astype(F32) * math.log(ratio))
    return jnp.where(distance % 2 == 0, size, -size)


def stencils(u, axis):
    n = u.shape[axis]
    plus_one = pltpu.roll(u, n - 1, axis)
    minus_one = pltpu.roll(u, 1, axis)
    plus_two = pltpu.roll(u, n - 2, axis)
    minus_two = pltpu.roll(u, 2, axis)
    first = FIRST_NEAR * (plus_one - minus_one) + FIRST_FAR * (plus_two - minus_two)
    second = SECOND_NEAR * (plus_one - 2.0 * u + minus_one) + SECOND_FAR * (
        plus_two - 2.0 * u + minus_two
    )
    return first, second


def iota(shape, axis):
    return lax.broadcasted_iota(jnp.int32, shape, axis)


def split(a):
    high = a.astype(BF16)
    return high, (a - high.astype(F32)).astype(BF16)


def dot(a, b):
    return jnp.dot(a, b, preferred_element_type=F32)


def dot3(a, b):
    ah, al = split(a)
    bh, bl = split(b)
    return dot(ah, bh) + dot(al, bh) + dot(ah, bl)


def kernel(
    nx, ny, v_ref, dx_ref, dy_ref, dxx_ref, dyy_ref, u_ref, xl, xr, yl, yr, load_sem, send, recv, ready
):
    ix = lax.axis_index("gx")
    iy = lax.axis_index("gy")
    up = {"gx": lax.rem(ix + 1, nx)}
    down = {"gx": lax.rem(ix + nx - 1, nx)}
    right = {"gy": lax.rem(iy + 1, ny)}
    left = {"gy": lax.rem(iy + ny - 1, ny)}
    rows, cols = u_ref.shape
    first = ix == 0
    last = ix == nx - 1
    odd = lax.rem(iy, 2)

    def signal(semaphore, other):
        pl.semaphore_signal(semaphore, inc=1, device_id=other, device_id_type=MESH)

    def remote(k, src, dst, other):
        return pltpu.make_async_remote_copy(
            src_ref=src,
            dst_ref=dst,
            send_sem=send.at[k],
            recv_sem=recv.at[k],
            device_id=other,
            device_id_type=MESH,
        )

    barrier = pltpu.get_barrier_semaphore()
    signal(barrier, down)
    pl.when(jnp.logical_not(last))(lambda: signal(barrier, up))

    @pl.when(odd == 1)
    def _():
        signal(barrier, left)
        signal(barrier, right)

    load = pltpu.make_async_copy(v_ref.at[0], u_ref, load_sem)
    to_up = remote(0, v_ref.at[0, pl.ds(rows - HALO, HALO), :], xl, up)
    to_down = remote(1, v_ref.at[0, pl.ds(0, HALO), :], xr, down)
    to_right = remote(2, v_ref.at[0, :, pl.ds(cols - 128, 128)], yl, right)
    to_left = remote(3, v_ref.at[0, :, pl.ds(0, 128)], yr, left)

    pl.semaphore_wait(barrier, jnp.where(first, 1, 2) + 2 * (1 - odd))
    to_up.start()
    load.start()
    pl.when(last)(lambda: signal(ready.at[2], up))
    pl.when(jnp.logical_not(first))(lambda: to_down.start())

    @pl.when(odd == 0)
    def _():
        signal(ready.at[0], right)
        signal(ready.at[1], left)

    @pl.when(odd == 1)
    def _():
        pl.semaphore_wait(ready.at[0], 1)
        pl.semaphore_wait(ready.at[1], 1)

    to_right.start()
    to_left.start()

    load.wait()
    u = u_ref[...]
    row = iota((rows, cols), 0)
    col = iota((rows, cols), 1)
    inner = (row >= 2) & (row < rows - 2)
    rx = [jnp.where(inner, s, 0.0) for s in stencils(u, 0)]
    distance = jnp.abs(iota((rows, rows), 0) - iota((rows, rows), 1))
    for out, c, s in zip((dx_ref, dxx_ref), COUPLINGS, rx):
        out[0] = dot3(powers(c, distance), s)
    inner = (col >= 2) & (col < cols - 2)
    ry = [jnp.where(inner, s, 0.0) for s in stencils(u, 1)]
    distance = jnp.abs(iota((cols, cols), 0) - iota((cols, cols), 1))
    fy = [dot3(s, powers(c, distance)) for c, s in zip(COUPLINGS, ry)]

    edge = HALO + 8
    place = iota((edge, cols), 0)
    tail = iota((HALO, cols), 0)
    below = []
    above = []
    for c in COUPLINGS:
        _, scale = green(c)
        below.append(
            (
                jnp.where((place >= 2) & (place <= HALO), powers(c, jnp.abs(HALO - place)), 0.0) / scale,
                powers(c, tail),
                powers(c, jnp.abs(tail - 1)),
            )
        )
        above.append(
            (
                jnp.where((place >= 7) & (place < edge - 2), powers(c, jnp.abs(place - 7)), 0.0) / scale,
                powers(c, HALO - 1 - tail),
                powers(c, jnp.abs(HALO - 2 - tail)),
            )
        )
    lane = iota((rows, 128), 1)
    source = iota((128, 128), 0)
    target = iota((128, 128), 1)
    sides = [
        [split(powers(c, jnp.abs(target - source + shift))) for c in COUPLINGS] for shift in (64, -64)
    ]
    near = [pltpu.roll(u[:, :128], 64, 1), pltpu.roll(u[:, cols - 128 :], 64, 1)]

    def multiply(a, b):
        ah, al = split(a)
        return dot(ah, b[0]) + dot(al, b[0]) + dot(ah, b[1])

    to_right.wait_recv()
    to_left.wait_recv()
    lower = stencils(jnp.where(lane < 64, pltpu.roll(yl[...], 64, 1), near[0]), 1)
    upper = stencils(jnp.where(lane < 64, near[1], pltpu.roll(yr[...], 64, 1)), 1)
    for k, out in enumerate((dy_ref, dyy_ref)):
        low = jnp.where((lane >= 2) & (lane < 66), lower[k], 0.0)
        high = jnp.where((lane >= 62) & (lane < 126), upper[k], 0.0)
        out[0] = fy[k] + jnp.concatenate(
            [multiply(low, sides[0][k]), multiply(high, sides[1][k])], axis=1
        )

    @pl.when(first)
    def _():
        pl.semaphore_wait(ready.at[2], 1)
        to_down.start()

    to_down.wait_recv()
    upper = stencils(jnp.concatenate([u[rows - 8 :], xr[...]], axis=0), 0)
    for k, out in enumerate((dx_ref, dxx_ref)):
        weight, far, close = above[k]
        total = jnp.sum(weight * upper[k], axis=0, keepdims=True)
        out[0, pl.ds(rows - HALO, HALO), :] += far * total + close * upper[k][6:7]

    to_up.wait_recv()
    lower = stencils(jnp.concatenate([xl[...], u[:8]], axis=0), 0)
    for k, out in enumerate((dx_ref, dxx_ref)):
        weight, far, close = below[k]
        total = jnp.sum(weight * lower[k], axis=0, keepdims=True)
        out[0, pl.ds(0, HALO), :] += far * total + close * lower[k][HALO + 1 : HALO + 2]

    for copy in (to_up, to_down, to_right, to_left):
        copy.wait_send()


def writer(*refs):
    sources, targets, sem = refs[:4], refs[4:8], refs[8]
    copies = [pltpu.make_async_copy(s, t, sem.at[k]) for k, (s, t) in enumerate(zip(sources, targets))]
    for copy in copies:
        copy.start()
    for copy in copies:
        copy.wait()


def local(nx, ny, velocity):
    _, rows, cols = velocity.shape
    out = jax.ShapeDtypeStruct(velocity.shape, F32)
    fields = pl.pallas_call(
        functools.partial(kernel, nx, ny),
        out_shape=(pltpu.VMEM(velocity.shape, F32),) * 4,
        in_specs=[pl.BlockSpec(memory_space=pl.ANY)],
        out_specs=[pl.BlockSpec(memory_space=pltpu.VMEM)] * 4,
        scratch_shapes=[
            pltpu.VMEM((rows, cols), F32),
            pltpu.VMEM((HALO, cols), F32),
            pltpu.VMEM((HALO, cols), F32),
            pltpu.VMEM((rows, 128), F32),
            pltpu.VMEM((rows, 128), F32),
            pltpu.SemaphoreType.DMA,
            pltpu.SemaphoreType.DMA((4,)),
            pltpu.SemaphoreType.DMA((4,)),
            pltpu.SemaphoreType.REGULAR((3,)),
        ],
        compiler_params=pltpu.CompilerParams(collective_id=0, has_side_effects=True),
    )(velocity)
    return pl.pallas_call(
        writer,
        out_shape=(out,) * 4,
        in_specs=[pl.BlockSpec(memory_space=pltpu.VMEM)] * 4,
        out_specs=[pl.BlockSpec(memory_space=pl.ANY)] * 4,
        scratch_shapes=[pltpu.SemaphoreType.DMA((4,))],
    )(*[pltpu.with_memory_space_constraint(f, pltpu.VMEM) for f in fields])


def solution(mesh):
    placed = P(None, "gx", "gy")
    return jax.shard_map(
        functools.partial(local, mesh.shape["gx"], mesh.shape["gy"]),
        mesh=mesh,
        in_specs=(placed,),
        out_specs=(placed,) * 4,
        check_vma=False,
    )
```

```python
import functools
import math

import jax
import jax.numpy as jnp
from jax import lax
from jax.experimental import pallas as pl
from jax.experimental.pallas import tpu as pltpu
from jax.sharding import PartitionSpec as P

FIRST_NEAR = 7.0 / 9.0
FIRST_FAR = 1.0 / 36.0
SECOND_NEAR = 12.0 / 11.0
SECOND_FAR = 3.0 / 44.0
COUPLINGS = (1.0 / 3.0, 2.0 / 11.0)
MESH = pl.DeviceIdType.MESH
HALO = 24
F32 = jnp.float32
BF16 = jnp.bfloat16


def green(coupling):
    root = math.sqrt(1.0 - 4.0 * coupling * coupling)
    return (1.0 - root) / (2.0 * coupling), 1.0 / root


def powers(coupling, distance):
    ratio, scale = green(coupling)
    size = scale * jnp.exp(distance.astype(F32) * math.log(ratio))
    return jnp.where(distance % 2 == 0, size, -size)


def stencils(u, axis):
    n = u.shape[axis]
    plus_one = pltpu.roll(u, n - 1, axis)
    minus_one = pltpu.roll(u, 1, axis)
    plus_two = pltpu.roll(u, n - 2, axis)
    minus_two = pltpu.roll(u, 2, axis)
    first = FIRST_NEAR * (plus_one - minus_one) + FIRST_FAR * (plus_two - minus_two)
    second = SECOND_NEAR * (plus_one - 2.0 * u + minus_one) + SECOND_FAR * (
        plus_two - 2.0 * u + minus_two
    )
    return first, second


def iota(shape, axis):
    return lax.broadcasted_iota(jnp.int32, shape, axis)


def split(a):
    high = a.astype(BF16)
    return high, (a - high.astype(F32)).astype(BF16)


def dot(a, b):
    return jnp.dot(a, b, preferred_element_type=F32)


def dot3(a, b):
    ah, al = split(a)
    bh, bl = split(b)
    return dot(ah, bh) + dot(al, bh) + dot(ah, bl)


def kernel(
    nx, ny, v_ref, dx_ref, dy_ref, dxx_ref, dyy_ref, u_ref, xl, xr, yl, yr, load_sem, send, recv, ready
):
    ix = lax.axis_index("gx")
    iy = lax.axis_index("gy")
    up = {"gx": lax.rem(ix + 1, nx)}
    down = {"gx": lax.rem(ix + nx - 1, nx)}
    right = {"gy": lax.rem(iy + 1, ny)}
    left = {"gy": lax.rem(iy + ny - 1, ny)}
    rows, cols = u_ref.shape
    first = ix == 0
    last = ix == nx - 1
    before = ix == nx - 2
    odd = lax.rem(iy, 2)

    def signal(semaphore, other):
        pl.semaphore_signal(semaphore, inc=1, device_id=other, device_id_type=MESH)

    def remote(k, src, dst, other):
        return pltpu.make_async_remote_copy(
            src_ref=src,
            dst_ref=dst,
            send_sem=send.at[k],
            recv_sem=recv.at[k],
            device_id=other,
            device_id_type=MESH,
        )

    barrier = pltpu.get_barrier_semaphore()
    signal(barrier, down)
    pl.when(ix < nx - 2)(lambda: signal(barrier, up))

    @pl.when((odd == 1) & (ix < nx - 1))
    def _():
        signal(barrier, left)
        signal(barrier, right)

    load = pltpu.make_async_copy(v_ref.at[0], u_ref, load_sem)
    to_up = remote(0, v_ref.at[0, pl.ds(rows - HALO, HALO), :], xl, up)
    to_down = remote(1, v_ref.at[0, pl.ds(0, HALO), :], xr, down)
    to_right = remote(2, v_ref.at[0, :, pl.ds(cols - 128, 128)], yl, right)
    to_left = remote(3, v_ref.at[0, :, pl.ds(0, 128)], yr, left)

    def answer_sides():
        signal(ready.at[0], right)
        signal(ready.at[1], left)

    def await_sides():
        pl.semaphore_wait(ready.at[0], 1)
        pl.semaphore_wait(ready.at[1], 1)

    along_x = jnp.where(first | last, 1, 2)
    along_y = jnp.where(last, 0, 2 * (1 - odd))
    pl.semaphore_wait(barrier, along_x + along_y)
    to_up.start()
    load.start()
    pl.when(last)(lambda: signal(ready.at[2], up))

    @pl.when(jnp.logical_not(last))
    def _():
        pl.when(jnp.logical_not(first))(lambda: to_down.start())
        pl.when(odd == 0)(answer_sides)

        @pl.when(odd == 1)
        def _():
            await_sides()

            @pl.when(before)
            def _():
                answer_sides()
                signal(ready.at[3], up)

        to_right.start()
        to_left.start()

    load.wait()
    u = u_ref[...]
    row = iota((rows, cols), 0)
    col = iota((rows, cols), 1)
    inner = (row >= 2) & (row < rows - 2)
    rx = [jnp.where(inner, s, 0.0) for s in stencils(u, 0)]
    distance = jnp.abs(iota((rows, rows), 0) - iota((rows, rows), 1))
    for out, c, s in zip((dx_ref, dxx_ref), COUPLINGS, rx):
        out[0] = dot3(powers(c, distance), s)
    inner = (col >= 2) & (col < cols - 2)
    ry = [jnp.where(inner, s, 0.0) for s in stencils(u, 1)]
    distance = jnp.abs(iota((cols, cols), 0) - iota((cols, cols), 1))
    fy = [dot3(s, powers(c, distance)) for c, s in zip(COUPLINGS, ry)]

    edge = HALO + 8
    place = iota((edge, cols), 0)
    tail = iota((HALO, cols), 0)
    below = []
    above = []
    for c in COUPLINGS:
        _, scale = green(c)
        below.append(
            (
                jnp.where((place >= 2) & (place <= HALO), powers(c, jnp.abs(HALO - place)), 0.0) / scale,
                powers(c, tail),
                powers(c, jnp.abs(tail - 1)),
            )
        )
        above.append(
            (
                jnp.where((place >= 7) & (place < edge - 2), powers(c, jnp.abs(place - 7)), 0.0) / scale,
                powers(c, HALO - 1 - tail),
                powers(c, jnp.abs(HALO - 2 - tail)),
            )
        )
    lane = iota((rows, 128), 1)
    source = iota((128, 128), 0)
    target = iota((128, 128), 1)
    sides = [
        [split(powers(c, jnp.abs(target - source + shift))) for c in COUPLINGS] for shift in (64, -64)
    ]
    near = [pltpu.roll(u[:, :128], 64, 1), pltpu.roll(u[:, cols - 128 :], 64, 1)]

    def multiply(a, b):
        ah, al = split(a)
        return dot(ah, b[0]) + dot(al, b[0]) + dot(ah, b[1])

    @pl.when(before & (odd == 0))
    def _():
        await_sides()
        signal(ready.at[3], up)

    @pl.when(last)
    def _():
        pl.semaphore_wait(ready.at[3], 1)
        to_right.start()
        to_left.start()
        to_down.start()

    to_right.wait_recv()
    to_left.wait_recv()
    lower = stencils(jnp.where(lane < 64, pltpu.roll(yl[...], 64, 1), near[0]), 1)
    upper = stencils(jnp.where(lane < 64, near[1], pltpu.roll(yr[...], 64, 1)), 1)
    for k, out in enumerate((dy_ref, dyy_ref)):
        low = jnp.where((lane >= 2) & (lane < 66), lower[k], 0.0)
        high = jnp.where((lane >= 62) & (lane < 126), upper[k], 0.0)
        out[0] = fy[k] + jnp.concatenate(
            [multiply(low, sides[0][k]), multiply(high, sides[1][k])], axis=1
        )

    @pl.when(first)
    def _():
        pl.semaphore_wait(ready.at[2], 1)
        to_down.start()

    to_down.wait_recv()
    upper = stencils(jnp.concatenate([u[rows - 8 :], xr[...]], axis=0), 0)
    for k, out in enumerate((dx_ref, dxx_ref)):
        weight, far, close = above[k]
        total = jnp.sum(weight * upper[k], axis=0, keepdims=True)
        out[0, pl.ds(rows - HALO, HALO), :] += far * total + close * upper[k][6:7]

    to_up.wait_recv()
    lower = stencils(jnp.concatenate([xl[...], u[:8]], axis=0), 0)
    for k, out in enumerate((dx_ref, dxx_ref)):
        weight, far, close = below[k]
        total = jnp.sum(weight * lower[k], axis=0, keepdims=True)
        out[0, pl.ds(0, HALO), :] += far * total + close * lower[k][HALO + 1 : HALO + 2]

    for copy in (to_up, to_down, to_right, to_left):
        copy.wait_send()


def writer(*refs):
    sources, targets, sem = refs[:4], refs[4:8], refs[8]
    copies = [pltpu.make_async_copy(s, t, sem.at[k]) for k, (s, t) in enumerate(zip(sources, targets))]
    for copy in copies:
        copy.start()
    for copy in copies:
        copy.wait()


def local(nx, ny, velocity):
    _, rows, cols = velocity.shape
    out = jax.ShapeDtypeStruct(velocity.shape, F32)
    fields = pl.pallas_call(
        functools.partial(kernel, nx, ny),
        out_shape=(pltpu.VMEM(velocity.shape, F32),) * 4,
        in_specs=[pl.BlockSpec(memory_space=pl.ANY)],
        out_specs=[pl.BlockSpec(memory_space=pltpu.VMEM)] * 4,
        scratch_shapes=[
            pltpu.VMEM((rows, cols), F32),
            pltpu.VMEM((HALO, cols), F32),
            pltpu.VMEM((HALO, cols), F32),
            pltpu.VMEM((rows, 128), F32),
            pltpu.VMEM((rows, 128), F32),
            pltpu.SemaphoreType.DMA,
            pltpu.SemaphoreType.DMA((4,)),
            pltpu.SemaphoreType.DMA((4,)),
            pltpu.SemaphoreType.REGULAR((4,)),
        ],
        compiler_params=pltpu.CompilerParams(collective_id=0, has_side_effects=True),
    )(velocity)
    return pl.pallas_call(
        writer,
        out_shape=(out,) * 4,
        in_specs=[pl.BlockSpec(memory_space=pltpu.VMEM)] * 4,
        out_specs=[pl.BlockSpec(memory_space=pl.ANY)] * 4,
        scratch_shapes=[pltpu.SemaphoreType.DMA((4,))],
    )(*[pltpu.with_memory_space_constraint(f, pltpu.VMEM) for f in fields])


def solution(mesh):
    placed = P(None, "gx", "gy")
    return jax.shard_map(
        functools.partial(local, mesh.shape["gx"], mesh.shape["gy"]),
        mesh=mesh,
        in_specs=(placed,),
        out_specs=(placed,) * 4,
        check_vma=False,
    )
```

```python
import functools
import math

import jax
import jax.numpy as jnp
from jax import lax
from jax.experimental import pallas as pl
from jax.experimental.pallas import tpu as pltpu
from jax.sharding import PartitionSpec as P

FIRST_NEAR = 7.0 / 9.0
FIRST_FAR = 1.0 / 36.0
SECOND_NEAR = 12.0 / 11.0
SECOND_FAR = 3.0 / 44.0
COUPLINGS = (1.0 / 3.0, 2.0 / 11.0)
MESH = pl.DeviceIdType.MESH
HALO = 24
F32 = jnp.float32
BF16 = jnp.bfloat16


def green(coupling):
    root = math.sqrt(1.0 - 4.0 * coupling * coupling)
    return (1.0 - root) / (2.0 * coupling), 1.0 / root


def powers(coupling, distance):
    ratio, scale = green(coupling)
    size = scale * jnp.exp(distance.astype(F32) * math.log(ratio))
    return jnp.where(distance % 2 == 0, size, -size)


def stencils(u, axis):
    n = u.shape[axis]
    plus_one = pltpu.roll(u, n - 1, axis)
    minus_one = pltpu.roll(u, 1, axis)
    plus_two = pltpu.roll(u, n - 2, axis)
    minus_two = pltpu.roll(u, 2, axis)
    first = FIRST_NEAR * (plus_one - minus_one) + FIRST_FAR * (plus_two - minus_two)
    second = SECOND_NEAR * (plus_one - 2.0 * u + minus_one) + SECOND_FAR * (
        plus_two - 2.0 * u + minus_two
    )
    return first, second


def iota(shape, axis):
    return lax.broadcasted_iota(jnp.int32, shape, axis)


def split(a):
    high = a.astype(BF16)
    return high, (a - high.astype(F32)).astype(BF16)


def dot(a, b):
    return jnp.dot(a, b, preferred_element_type=F32)


def kernel(
    nx,
    ny,
    v_ref,
    dx_ref,
    dy_ref,
    dxx_ref,
    dyy_ref,
    edge_ref,
    weight_ref,
    u_ref,
    xr,
    yl,
    yr,
    load_sem,
    send,
    recv,
    ready,
):
    ix = lax.axis_index("gx")
    iy = lax.axis_index("gy")
    up = {"gx": jnp.where(ix == nx - 1, 0, ix + 1)}
    down = {"gx": jnp.where(ix == 0, nx - 1, ix - 1)}
    right = {"gy": jnp.where(iy == ny - 1, 0, iy + 1)}
    left = {"gy": jnp.where(iy == 0, ny - 1, iy - 1)}
    rows, cols = u_ref.shape
    first = ix == 0
    last = ix == nx - 1
    before = ix == nx - 2
    odd = lax.rem(iy, 2)

    def signal(semaphore, other):
        pl.semaphore_signal(semaphore, inc=1, device_id=other, device_id_type=MESH)

    def remote(k, src, dst, other):
        return pltpu.make_async_remote_copy(
            src_ref=src,
            dst_ref=dst,
            send_sem=send.at[k],
            recv_sem=recv.at[k],
            device_id=other,
            device_id_type=MESH,
        )

    load = pltpu.make_async_copy(v_ref.at[0], u_ref, load_sem)
    to_up = remote(0, v_ref.at[0, pl.ds(rows - HALO, HALO), :], edge_ref.at[pl.ds(0, HALO), :], up)
    to_down = remote(1, v_ref.at[0, pl.ds(0, HALO), :], xr, down)
    to_right = remote(2, v_ref.at[0, :, pl.ds(cols - 128, 128)], yl, right)
    to_left = remote(3, v_ref.at[0, :, pl.ds(0, 128)], yr, left)

    barrier = pltpu.get_barrier_semaphore()
    signal(barrier, down)

    @pl.when(last)
    def _():
        pl.semaphore_wait(barrier, 1)
        to_up.start()
        signal(ready.at[2], up)

    def greet_sides():
        signal(barrier, left)
        signal(barrier, right)

    def answer_sides():
        signal(ready.at[0], right)
        signal(ready.at[1], left)

    @pl.when(jnp.logical_not(last))
    def _():
        pl.when(jnp.logical_not(before))(lambda: signal(barrier, up))
        pl.when((odd == 1) & jnp.logical_not(before))(greet_sides)
        pl.semaphore_wait(barrier, jnp.where(first, 1, 2) + 2 * (1 - odd))
        to_up.start()

        @pl.when(before)
        def _():
            signal(ready.at[3], up)
            pl.when(odd == 0)(lambda: signal(ready.at[4], up))
            pl.when(odd == 1)(greet_sides)

        pl.when(jnp.logical_not(first))(lambda: to_down.start())
        pl.when(odd == 0)(answer_sides)

        @pl.when(odd == 1)
        def _():
            pl.semaphore_wait(ready.at[0], 1)
            pl.semaphore_wait(ready.at[1], 1)
            pl.when(before)(lambda: signal(ready.at[4], up))

        to_right.start()
        to_left.start()

    load.start()
    distance = jnp.abs(iota((rows, rows), 0) - iota((rows, rows), 1))
    across = [split(powers(c, distance)) for c in COUPLINGS]
    distance = jnp.abs(iota((cols, cols), 0) - iota((cols, cols), 1))
    along = [split(powers(c, distance)) for c in COUPLINGS]
    edge = HALO + 8
    place = iota((edge, cols), 0)
    tail = iota((HALO, cols), 0)
    above = []
    for k, c in enumerate(COUPLINGS):
        _, scale = green(c)
        weight_ref[k, pl.ds(0, edge), :] = (
            jnp.where((place >= 2) & (place <= HALO), powers(c, jnp.abs(HALO - place)), 0.0) / scale
        )
        weight_ref[k, pl.ds(edge, HALO), :] = powers(c, tail)
        weight_ref[k, pl.ds(edge + HALO, HALO), :] = powers(c, jnp.abs(tail - 1))
        above.append(
            (
                jnp.where((place >= 7) & (place < edge - 2), powers(c, jnp.abs(place - 7)), 0.0) / scale,
                powers(c, HALO - 1 - tail),
                powers(c, jnp.abs(HALO - 2 - tail)),
            )
        )
    lane = iota((rows, 128), 1)
    source = iota((128, 128), 0)
    target = iota((128, 128), 1)
    sides = [
        [split(powers(c, jnp.abs(target - source + shift))) for c in COUPLINGS] for shift in (64, -64)
    ]
    def multiply(a, b):
        ah, al = split(a)
        return dot(ah, b[0]) + dot(al, b[0]) + dot(ah, b[1])

    load.wait()
    u = u_ref[...]
    edge_ref[pl.ds(HALO, 8), :] = u[:8]
    near = [pltpu.roll(u[:, :128], 64, 1), pltpu.roll(u[:, cols - 128 :], 64, 1)]

    row = iota((rows, cols), 0)
    col = iota((rows, cols), 1)
    inner = (row >= 2) & (row < rows - 2)
    for out, g, s in zip((dx_ref, dxx_ref), across, stencils(u, 0)):
        high, low = split(jnp.where(inner, s, 0.0))
        out[0] = dot(g[0], high) + dot(g[1], high) + dot(g[0], low)
    inner = (col >= 2) & (col < cols - 2)
    fy = [multiply(jnp.where(inner, s, 0.0), g) for g, s in zip(along, stencils(u, 1))]

    @pl.when(last)
    def _():
        pl.semaphore_wait(ready.at[3], 1)
        to_down.start()
        pl.semaphore_wait(ready.at[4], 1)
        to_right.start()
        to_left.start()

    to_right.wait_recv()
    to_left.wait_recv()
    lower = stencils(jnp.where(lane < 64, pltpu.roll(yl[...], 64, 1), near[0]), 1)
    upper = stencils(jnp.where(lane < 64, near[1], pltpu.roll(yr[...], 64, 1)), 1)
    for k, out in enumerate((dy_ref, dyy_ref)):
        low = jnp.where((lane >= 2) & (lane < 66), lower[k], 0.0)
        high = jnp.where((lane >= 62) & (lane < 126), upper[k], 0.0)
        out[0] = fy[k] + jnp.concatenate(
            [multiply(low, sides[0][k]), multiply(high, sides[1][k])], axis=1
        )

    @pl.when(first)
    def _():
        pl.semaphore_wait(ready.at[2], 1)
        remote(1, u_ref.at[pl.ds(0, HALO), :], xr, down).start()

    to_down.wait_recv()
    upper = stencils(jnp.concatenate([u[rows - 8 :], xr[...]], axis=0), 0)
    for k, out in enumerate((dx_ref, dxx_ref)):
        weight, far, close = above[k]
        total = jnp.sum(weight * upper[k], axis=0, keepdims=True)
        out[0, pl.ds(rows - HALO, HALO), :] += far * total + close * upper[k][6:7]

    to_up.wait_recv()
    for copy in (to_up, to_down, to_right, to_left):
        copy.wait_send()


def finish(
    dx_in, dy_in, dxx_in, dyy_in, edge_ref, weight_ref, dx_ref, dy_ref, dxx_ref, dyy_ref, low, sem
):
    rest = pl.ds(HALO, dx_in.shape[1] - HALO)
    copies = [
        pltpu.make_async_copy(dy_in, dy_ref, sem.at[0]),
        pltpu.make_async_copy(dyy_in, dyy_ref, sem.at[1]),
        pltpu.make_async_copy(dx_in.at[0, rest, :], dx_ref.at[0, rest, :], sem.at[2]),
        pltpu.make_async_copy(dxx_in.at[0, rest, :], dxx_ref.at[0, rest, :], sem.at[3]),
    ]
    for copy in copies:
        copy.start()
    edge = HALO + 8
    head = pl.ds(0, HALO)
    lower = stencils(edge_ref[...], 0)
    for k, (part, out) in enumerate(((dx_in, dx_ref), (dxx_in, dxx_ref))):
        total = jnp.sum(weight_ref[k, pl.ds(0, edge), :] * lower[k], axis=0, keepdims=True)
        low[k] = (
            part[0, head, :]
            + weight_ref[k, pl.ds(edge, HALO), :] * total
            + weight_ref[k, pl.ds(edge + HALO, HALO), :] * lower[k][HALO + 1 : HALO + 2]
        )
        copy = pltpu.make_async_copy(low.at[k], out.at[0, head, :], sem.at[4 + k])
        copy.start()
        copies.append(copy)
    for copy in copies:
        copy.wait()


def local(nx, ny, velocity):
    _, rows, cols = velocity.shape
    out = jax.ShapeDtypeStruct(velocity.shape, F32)
    vmem = pl.BlockSpec(memory_space=pltpu.VMEM)
    anywhere = pl.BlockSpec(memory_space=pl.ANY)
    fields = pl.pallas_call(
        functools.partial(kernel, nx, ny),
        out_shape=(pltpu.VMEM(velocity.shape, F32),) * 4
        + (pltpu.VMEM((HALO + 8, cols), F32), pltpu.VMEM((2, 3 * HALO + 8, cols), F32)),
        in_specs=[anywhere],
        out_specs=[vmem] * 6,
        scratch_shapes=[
            pltpu.VMEM((rows, cols), F32),
            pltpu.VMEM((HALO, cols), F32),
            pltpu.VMEM((rows, 128), F32),
            pltpu.VMEM((rows, 128), F32),
            pltpu.SemaphoreType.DMA,
            pltpu.SemaphoreType.DMA((4,)),
            pltpu.SemaphoreType.DMA((4,)),
            pltpu.SemaphoreType.REGULAR((5,)),
        ],
        compiler_params=pltpu.CompilerParams(collective_id=0, has_side_effects=True),
    )(velocity)
    return pl.pallas_call(
        finish,
        out_shape=(out,) * 4,
        in_specs=[vmem] * 6,
        out_specs=[anywhere] * 4,
        scratch_shapes=[pltpu.VMEM((2, HALO, cols), F32), pltpu.SemaphoreType.DMA((6,))],
    )(*[pltpu.with_memory_space_constraint(f, pltpu.VMEM) for f in fields])


def solution(mesh):
    placed = P(None, "gx", "gy")
    return jax.shard_map(
        functools.partial(local, mesh.shape["gx"], mesh.shape["gy"]),
        mesh=mesh,
        in_specs=(placed,),
        out_specs=(placed,) * 4,
        check_vma=False,
    )
```

```python
import functools
import math

import jax
import jax.numpy as jnp
from jax import lax
from jax.experimental import pallas as pl
from jax.experimental.pallas import tpu as pltpu
from jax.sharding import PartitionSpec as P

FIRST_NEAR = 7.0 / 9.0
FIRST_FAR = 1.0 / 36.0
SECOND_NEAR = 12.0 / 11.0
SECOND_FAR = 3.0 / 44.0
COUPLINGS = (1.0 / 3.0, 2.0 / 11.0)
MESH = pl.DeviceIdType.MESH
HALO = 24
F32 = jnp.float32
BF16 = jnp.bfloat16


def green(coupling):
    root = math.sqrt(1.0 - 4.0 * coupling * coupling)
    return (1.0 - root) / (2.0 * coupling), 1.0 / root


def powers(coupling, distance):
    ratio, scale = green(coupling)
    size = scale * jnp.exp(distance.astype(F32) * math.log(ratio))
    return jnp.where(distance % 2 == 0, size, -size)


def stencils(u, axis):
    n = u.shape[axis]
    plus_one = pltpu.roll(u, n - 1, axis)
    minus_one = pltpu.roll(u, 1, axis)
    plus_two = pltpu.roll(u, n - 2, axis)
    minus_two = pltpu.roll(u, 2, axis)
    first = FIRST_NEAR * (plus_one - minus_one) + FIRST_FAR * (plus_two - minus_two)
    second = SECOND_NEAR * (plus_one - 2.0 * u + minus_one) + SECOND_FAR * (
        plus_two - 2.0 * u + minus_two
    )
    return first, second


def iota(shape, axis):
    return lax.broadcasted_iota(jnp.int32, shape, axis)


def split(a):
    high = a.astype(BF16)
    return high, (a - high.astype(F32)).astype(BF16)


def dot(a, b):
    return jnp.dot(a, b, preferred_element_type=F32)


def kernel(
    nx,
    ny,
    v_ref,
    dx_ref,
    dy_ref,
    dxx_ref,
    dyy_ref,
    edge_ref,
    weight_ref,
    u_ref,
    xr,
    yl,
    yr,
    pool,
    load_sem,
    send,
    recv,
    ready,
):
    ix = lax.axis_index("gx")
    iy = lax.axis_index("gy")
    up = {"gx": jnp.where(ix == nx - 1, 0, ix + 1)}
    down = {"gx": jnp.where(ix == 0, nx - 1, ix - 1)}
    right = {"gy": jnp.where(iy == ny - 1, 0, iy + 1)}
    left = {"gy": jnp.where(iy == 0, ny - 1, iy - 1)}
    rows, cols = u_ref.shape
    first = ix == 0
    last = ix == nx - 1
    before = ix == nx - 2
    odd = lax.rem(iy, 2)

    def signal(semaphore, other):
        pl.semaphore_signal(semaphore, inc=1, device_id=other, device_id_type=MESH)

    def remote(k, src, dst, other):
        return pltpu.make_async_remote_copy(
            src_ref=src,
            dst_ref=dst,
            send_sem=send,
            recv_sem=recv.at[k],
            device_id=other,
            device_id_type=MESH,
        )

    def take(count, semaphore):
        part = pool.at[pl.ds(0, count), :]
        pltpu.make_async_copy(part, part, semaphore).wait()

    load = pltpu.make_async_copy(v_ref.at[0], u_ref, load_sem)
    to_up = remote(0, v_ref.at[0, pl.ds(rows - HALO, HALO), :], edge_ref.at[pl.ds(0, HALO), :], up)
    to_down = remote(1, v_ref.at[0, pl.ds(0, HALO), :], xr, down)
    to_right = remote(1, v_ref.at[0, :, pl.ds(cols - 128, 128)], yl, right)
    to_left = remote(1, v_ref.at[0, :, pl.ds(0, 128)], yr, left)

    barrier = pltpu.get_barrier_semaphore()
    signal(barrier, down)

    @pl.when(last)
    def _():
        pl.semaphore_wait(barrier, 1)
        to_up.start()
        signal(ready.at[1], up)

    def greet_sides():
        signal(barrier, left)
        signal(barrier, right)

    def answer_sides():
        signal(ready.at[0], right)
        signal(ready.at[0], left)

    @pl.when(jnp.logical_not(last))
    def _():
        pl.when(jnp.logical_not(before))(lambda: signal(barrier, up))
        pl.when((odd == 1) & jnp.logical_not(before))(greet_sides)
        pl.semaphore_wait(barrier, jnp.where(first, 1, 2) + 2 * (1 - odd))
        to_up.start()

        @pl.when(before)
        def _():
            signal(ready.at[0], up)
            pl.when(odd == 0)(lambda: signal(ready.at[1], up))
            pl.when(odd == 1)(greet_sides)

        pl.when(jnp.logical_not(first))(lambda: to_down.start())
        pl.when(odd == 0)(answer_sides)

        @pl.when(odd == 1)
        def _():
            pl.semaphore_wait(ready.at[0], 2)
            pl.when(before)(lambda: signal(ready.at[1], up))

        to_right.start()
        to_left.start()

    load.start()
    distance = jnp.abs(iota((rows, rows), 0) - iota((rows, rows), 1))
    across = [split(powers(c, distance)) for c in COUPLINGS]
    distance = jnp.abs(iota((cols, cols), 0) - iota((cols, cols), 1))
    along = [split(powers(c, distance)) for c in COUPLINGS]
    edge = HALO + 8
    place = iota((edge, cols), 0)
    tail = iota((HALO, cols), 0)
    above = []
    for k, c in enumerate(COUPLINGS):
        _, scale = green(c)
        weight_ref[k, pl.ds(0, edge), :] = (
            jnp.where((place >= 2) & (place <= HALO), powers(c, jnp.abs(HALO - place)), 0.0) / scale
        )
        weight_ref[k, pl.ds(edge, HALO), :] = powers(c, tail)
        weight_ref[k, pl.ds(edge + HALO, HALO), :] = powers(c, jnp.abs(tail - 1))
        above.append(
            (
                jnp.where((place >= 7) & (place < edge - 2), powers(c, jnp.abs(place - 7)), 0.0) / scale,
                powers(c, HALO - 1 - tail),
                powers(c, jnp.abs(HALO - 2 - tail)),
            )
        )
    lane = iota((rows, 128), 1)
    source = iota((128, 128), 0)
    target = iota((128, 128), 1)
    sides = [
        [split(powers(c, jnp.abs(target - source + shift))) for c in COUPLINGS] for shift in (64, -64)
    ]

    def multiply(a, b):
        ah, al = split(a)
        return dot(ah, b[0]) + dot(al, b[0]) + dot(ah, b[1])

    load.wait()
    u = u_ref[...]
    edge_ref[pl.ds(HALO, 8), :] = u[:8]
    near = [pltpu.roll(u[:, :128], 64, 1), pltpu.roll(u[:, cols - 128 :], 64, 1)]

    row = iota((rows, cols), 0)
    col = iota((rows, cols), 1)
    inner = (row >= 2) & (row < rows - 2)
    for out, g, s in zip((dx_ref, dxx_ref), across, stencils(u, 0)):
        high, low = split(jnp.where(inner, s, 0.0))
        out[0] = dot(g[0], high) + dot(g[1], high) + dot(g[0], low)
    inner = (col >= 2) & (col < cols - 2)
    fy = [multiply(jnp.where(inner, s, 0.0), g) for g, s in zip(along, stencils(u, 1))]

    @pl.when(last)
    def _():
        pl.semaphore_wait(ready.at[0], 1)
        to_down.start()
        pl.semaphore_wait(ready.at[1], 1)
        to_right.start()
        to_left.start()

    @pl.when(first)
    def _():
        pl.semaphore_wait(ready.at[1], 1)
        remote(1, u_ref.at[pl.ds(0, HALO), :], xr, down).start()

    take(rows + HALO, recv.at[1])
    lower = stencils(jnp.where(lane < 64, pltpu.roll(yl[...], 64, 1), near[0]), 1)
    upper = stencils(jnp.where(lane < 64, near[1], pltpu.roll(yr[...], 64, 1)), 1)
    for k, out in enumerate((dy_ref, dyy_ref)):
        low = jnp.where((lane >= 2) & (lane < 66), lower[k], 0.0)
        high = jnp.where((lane >= 62) & (lane < 126), upper[k], 0.0)
        out[0] = fy[k] + jnp.concatenate(
            [multiply(low, sides[0][k]), multiply(high, sides[1][k])], axis=1
        )

    upper = stencils(jnp.concatenate([u[rows - 8 :], xr[...]], axis=0), 0)
    for k, out in enumerate((dx_ref, dxx_ref)):
        weight, far, close = above[k]
        total = jnp.sum(weight * upper[k], axis=0, keepdims=True)
        out[0, pl.ds(rows - HALO, HALO), :] += far * total + close * upper[k][6:7]

    to_up.wait_recv()
    take(rows + 2 * HALO, send)


def finish(
    dx_in, dy_in, dxx_in, dyy_in, edge_ref, weight_ref, dx_ref, dy_ref, dxx_ref, dyy_ref, low, pool, sem
):
    rest = pl.ds(HALO, dx_in.shape[1] - HALO)
    copies = [
        pltpu.make_async_copy(dy_in, dy_ref, sem),
        pltpu.make_async_copy(dyy_in, dyy_ref, sem),
        pltpu.make_async_copy(dx_in.at[0, rest, :], dx_ref.at[0, rest, :], sem),
        pltpu.make_async_copy(dxx_in.at[0, rest, :], dxx_ref.at[0, rest, :], sem),
    ]
    for copy in copies:
        copy.start()
    edge = HALO + 8
    head = pl.ds(0, HALO)
    lower = stencils(edge_ref[...], 0)
    for k, (part, out) in enumerate(((dx_in, dx_ref), (dxx_in, dxx_ref))):
        total = jnp.sum(weight_ref[k, pl.ds(0, edge), :] * lower[k], axis=0, keepdims=True)
        low[k] = (
            part[0, head, :]
            + weight_ref[k, pl.ds(edge, HALO), :] * total
            + weight_ref[k, pl.ds(edge + HALO, HALO), :] * lower[k][HALO + 1 : HALO + 2]
        )
        pltpu.make_async_copy(low.at[k], out.at[0, head, :], sem).start()
    pltpu.make_async_copy(pool, pool, sem).wait()


def local(nx, ny, velocity):
    _, rows, cols = velocity.shape
    out = jax.ShapeDtypeStruct(velocity.shape, F32)
    vmem = pl.BlockSpec(memory_space=pltpu.VMEM)
    anywhere = pl.BlockSpec(memory_space=pl.ANY)
    fields = pl.pallas_call(
        functools.partial(kernel, nx, ny),
        out_shape=(pltpu.VMEM(velocity.shape, F32),) * 4
        + (pltpu.VMEM((HALO + 8, cols), F32), pltpu.VMEM((2, 3 * HALO + 8, cols), F32)),
        in_specs=[anywhere],
        out_specs=[vmem] * 6,
        scratch_shapes=[
            pltpu.VMEM((rows, cols), F32),
            pltpu.VMEM((HALO, cols), F32),
            pltpu.VMEM((rows, 128), F32),
            pltpu.VMEM((rows, 128), F32),
            pltpu.VMEM((rows + 2 * HALO, cols), F32),
            pltpu.SemaphoreType.DMA,
            pltpu.SemaphoreType.DMA,
            pltpu.SemaphoreType.DMA((2,)),
            pltpu.SemaphoreType.REGULAR((2,)),
        ],
        compiler_params=pltpu.CompilerParams(collective_id=0, has_side_effects=True),
    )(velocity)
    return pl.pallas_call(
        finish,
        out_shape=(out,) * 4,
        in_specs=[vmem] * 6,
        out_specs=[anywhere] * 4,
        scratch_shapes=[
            pltpu.VMEM((2, HALO, cols), F32),
            pltpu.VMEM((4 * rows, cols), F32),
            pltpu.SemaphoreType.DMA,
        ],
    )(*[pltpu.with_memory_space_constraint(f, pltpu.VMEM) for f in fields])


def solution(mesh):
    placed = P(None, "gx", "gy")
    return jax.shard_map(
        functools.partial(local, mesh.shape["gx"], mesh.shape["gy"]),
        mesh=mesh,
        in_specs=(placed,),
        out_specs=(placed,) * 4,
        check_vma=False,
    )
```

```python
import functools
import math

import jax
import jax.numpy as jnp
from jax import lax
from jax.experimental import pallas as pl
from jax.experimental.pallas import tpu as pltpu
from jax.sharding import PartitionSpec as P

FIRST_NEAR = 7.0 / 9.0
FIRST_FAR = 1.0 / 36.0
SECOND_NEAR = 12.0 / 11.0
SECOND_FAR = 3.0 / 44.0
COUPLINGS = (1.0 / 3.0, 2.0 / 11.0)
MESH = pl.DeviceIdType.MESH
HALO = 24
F32 = jnp.float32


def green(coupling):
    root = math.sqrt(1.0 - 4.0 * coupling * coupling)
    return (1.0 - root) / (2.0 * coupling), 1.0 / root


def powers(coupling, distance):
    ratio, scale = green(coupling)
    size = scale * jnp.exp(distance.astype(F32) * math.log(ratio))
    return jnp.where(distance % 2 == 0, size, -size)


def stencils(u, axis):
    n = u.shape[axis]
    plus_one = pltpu.roll(u, n - 1, axis)
    minus_one = pltpu.roll(u, 1, axis)
    plus_two = pltpu.roll(u, n - 2, axis)
    minus_two = pltpu.roll(u, 2, axis)
    first = FIRST_NEAR * (plus_one - minus_one) + FIRST_FAR * (plus_two - minus_two)
    second = SECOND_NEAR * (plus_one - 2.0 * u + minus_one) + SECOND_FAR * (
        plus_two - 2.0 * u + minus_two
    )
    return first, second


def iota(shape, axis):
    return lax.broadcasted_iota(jnp.int32, shape, axis)


def dot(a, b):
    return jnp.dot(a, b, precision=lax.Precision.HIGHEST, preferred_element_type=F32)


def kernel(
    nx,
    ny,
    v_ref,
    dx_ref,
    dy_ref,
    dxx_ref,
    dyy_ref,
    edge_ref,
    weight_ref,
    u_ref,
    xr,
    yl,
    yr,
    pool,
    load_sem,
    send,
    recv,
    ready,
):
    ix = lax.axis_index("gx")
    iy = lax.axis_index("gy")
    up = {"gx": jnp.where(ix == nx - 1, 0, ix + 1)}
    down = {"gx": jnp.where(ix == 0, nx - 1, ix - 1)}
    right = {"gy": jnp.where(iy == ny - 1, 0, iy + 1)}
    left = {"gy": jnp.where(iy == 0, ny - 1, iy - 1)}
    rows, cols = u_ref.shape
    first = ix == 0
    last = ix == nx - 1
    before = ix == nx - 2
    odd = lax.rem(iy, 2)

    def signal(semaphore, other):
        pl.semaphore_signal(semaphore, inc=1, device_id=other, device_id_type=MESH)

    def remote(k, src, dst, other):
        return pltpu.make_async_remote_copy(
            src_ref=src,
            dst_ref=dst,
            send_sem=send,
            recv_sem=recv.at[k],
            device_id=other,
            device_id_type=MESH,
        )

    def take(count, semaphore):
        part = pool.at[pl.ds(0, count), :]
        pltpu.make_async_copy(part, part, semaphore).wait()

    load = pltpu.make_async_copy(v_ref.at[0], u_ref, load_sem)
    to_up = remote(0, v_ref.at[0, pl.ds(rows - HALO, HALO), :], edge_ref.at[pl.ds(0, HALO), :], up)
    to_down = remote(1, v_ref.at[0, pl.ds(0, HALO), :], xr, down)
    to_right = remote(1, v_ref.at[0, :, pl.ds(cols - 128, 128)], yl, right)
    to_left = remote(1, v_ref.at[0, :, pl.ds(0, 128)], yr, left)

    barrier = pltpu.get_barrier_semaphore()
    signal(barrier, down)

    @pl.when(last)
    def _():
        pl.semaphore_wait(barrier, 1)
        to_up.start()
        signal(ready.at[1], up)

    def greet_sides():
        signal(barrier, left)
        signal(barrier, right)

    def answer_sides():
        signal(ready.at[0], right)
        signal(ready.at[0], left)

    @pl.when(jnp.logical_not(last))
    def _():
        pl.when(jnp.logical_not(before))(lambda: signal(barrier, up))
        pl.when((odd == 1) & jnp.logical_not(before))(greet_sides)
        pl.semaphore_wait(barrier, jnp.where(first, 1, 2) + 2 * (1 - odd))
        to_up.start()

        @pl.when(before)
        def _():
            signal(ready.at[0], up)
            pl.when(odd == 0)(lambda: signal(ready.at[1], up))
            pl.when(odd == 1)(greet_sides)

        pl.when(jnp.logical_not(first))(lambda: to_down.start())
        pl.when(odd == 0)(answer_sides)

        @pl.when(odd == 1)
        def _():
            pl.semaphore_wait(ready.at[0], 2)
            pl.when(before)(lambda: signal(ready.at[1], up))

        to_right.start()
        to_left.start()

    load.start()
    distance = jnp.abs(iota((rows, rows), 0) - iota((rows, rows), 1))
    across = [powers(c, distance) for c in COUPLINGS]
    distance = jnp.abs(iota((cols, cols), 0) - iota((cols, cols), 1))
    along = [powers(c, distance) for c in COUPLINGS]
    edge = HALO + 8
    place = iota((edge, cols), 0)
    tail = iota((HALO, cols), 0)
    above = []
    for k, c in enumerate(COUPLINGS):
        _, scale = green(c)
        weight_ref[k, pl.ds(0, edge), :] = (
            jnp.where((place >= 2) & (place <= HALO), powers(c, jnp.abs(HALO - place)), 0.0) / scale
        )
        weight_ref[k, pl.ds(edge, HALO), :] = powers(c, tail)
        weight_ref[k, pl.ds(edge + HALO, HALO), :] = powers(c, jnp.abs(tail - 1))
        above.append(
            (
                jnp.where((place >= 7) & (place < edge - 2), powers(c, jnp.abs(place - 7)), 0.0) / scale,
                powers(c, HALO - 1 - tail),
                powers(c, jnp.abs(HALO - 2 - tail)),
            )
        )
    lane = iota((rows, 128), 1)
    source = iota((128, 128), 0)
    target = iota((128, 128), 1)
    sides = [[powers(c, jnp.abs(target - source + shift)) for c in COUPLINGS] for shift in (64, -64)]

    load.wait()
    u = u_ref[...]
    edge_ref[pl.ds(HALO, 8), :] = u[:8]
    near = [pltpu.roll(u[:, :128], 64, 1), pltpu.roll(u[:, cols - 128 :], 64, 1)]

    row = iota((rows, cols), 0)
    col = iota((rows, cols), 1)
    inner = (row >= 2) & (row < rows - 2)
    for out, g, s in zip((dx_ref, dxx_ref), across, stencils(u, 0)):
        out[0] = dot(g, jnp.where(inner, s, 0.0))
    inner = (col >= 2) & (col < cols - 2)
    fy = [dot(jnp.where(inner, s, 0.0), g) for g, s in zip(along, stencils(u, 1))]

    @pl.when(last)
    def _():
        pl.semaphore_wait(ready.at[0], 1)
        to_down.start()
        pl.semaphore_wait(ready.at[1], 1)
        to_right.start()
        to_left.start()

    @pl.when(first)
    def _():
        pl.semaphore_wait(ready.at[1], 1)
        remote(1, u_ref.at[pl.ds(0, HALO), :], xr, down).start()

    take(rows + HALO, recv.at[1])
    lower = stencils(jnp.where(lane < 64, pltpu.roll(yl[...], 64, 1), near[0]), 1)
    upper = stencils(jnp.where(lane < 64, near[1], pltpu.roll(yr[...], 64, 1)), 1)
    for k, out in enumerate((dy_ref, dyy_ref)):
        low = jnp.where((lane >= 2) & (lane < 66), lower[k], 0.0)
        high = jnp.where((lane >= 62) & (lane < 126), upper[k], 0.0)
        out[0] = fy[k] + jnp.concatenate(
            [dot(low, sides[0][k]), dot(high, sides[1][k])], axis=1
        )

    upper = stencils(jnp.concatenate([u[rows - 8 :], xr[...]], axis=0), 0)
    for k, out in enumerate((dx_ref, dxx_ref)):
        weight, far, close = above[k]
        total = jnp.sum(weight * upper[k], axis=0, keepdims=True)
        out[0, pl.ds(rows - HALO, HALO), :] += far * total + close * upper[k][6:7]

    to_up.wait_recv()
    take(rows + 2 * HALO, send)


def finish(
    dx_in, dy_in, dxx_in, dyy_in, edge_ref, weight_ref, dx_ref, dy_ref, dxx_ref, dyy_ref, low, pool, sem
):
    rest = pl.ds(HALO, dx_in.shape[1] - HALO)
    copies = [
        pltpu.make_async_copy(dy_in, dy_ref, sem),
        pltpu.make_async_copy(dyy_in, dyy_ref, sem),
        pltpu.make_async_copy(dx_in.at[0, rest, :], dx_ref.at[0, rest, :], sem),
        pltpu.make_async_copy(dxx_in.at[0, rest, :], dxx_ref.at[0, rest, :], sem),
    ]
    for copy in copies:
        copy.start()
    edge = HALO + 8
    head = pl.ds(0, HALO)
    lower = stencils(edge_ref[...], 0)
    for k, (part, out) in enumerate(((dx_in, dx_ref), (dxx_in, dxx_ref))):
        total = jnp.sum(weight_ref[k, pl.ds(0, edge), :] * lower[k], axis=0, keepdims=True)
        low[k] = (
            part[0, head, :]
            + weight_ref[k, pl.ds(edge, HALO), :] * total
            + weight_ref[k, pl.ds(edge + HALO, HALO), :] * lower[k][HALO + 1 : HALO + 2]
        )
        pltpu.make_async_copy(low.at[k], out.at[0, head, :], sem).start()
    pltpu.make_async_copy(pool, pool, sem).wait()


def local(nx, ny, velocity):
    _, rows, cols = velocity.shape
    out = jax.ShapeDtypeStruct(velocity.shape, F32)
    vmem = pl.BlockSpec(memory_space=pltpu.VMEM)
    anywhere = pl.BlockSpec(memory_space=pl.ANY)
    fields = pl.pallas_call(
        functools.partial(kernel, nx, ny),
        out_shape=(pltpu.VMEM(velocity.shape, F32),) * 4
        + (pltpu.VMEM((HALO + 8, cols), F32), pltpu.VMEM((2, 3 * HALO + 8, cols), F32)),
        in_specs=[anywhere],
        out_specs=[vmem] * 6,
        scratch_shapes=[
            pltpu.VMEM((rows, cols), F32),
            pltpu.VMEM((HALO, cols), F32),
            pltpu.VMEM((rows, 128), F32),
            pltpu.VMEM((rows, 128), F32),
            pltpu.VMEM((rows + 2 * HALO, cols), F32),
            pltpu.SemaphoreType.DMA,
            pltpu.SemaphoreType.DMA,
            pltpu.SemaphoreType.DMA((2,)),
            pltpu.SemaphoreType.REGULAR((2,)),
        ],
        compiler_params=pltpu.CompilerParams(collective_id=0, has_side_effects=True),
    )(velocity)
    return pl.pallas_call(
        finish,
        out_shape=(out,) * 4,
        in_specs=[vmem] * 6,
        out_specs=[anywhere] * 4,
        scratch_shapes=[
            pltpu.VMEM((2, HALO, cols), F32),
            pltpu.VMEM((4 * rows, cols), F32),
            pltpu.SemaphoreType.DMA,
        ],
    )(*[pltpu.with_memory_space_constraint(f, pltpu.VMEM) for f in fields])


def solution(mesh):
    placed = P(None, "gx", "gy")
    return jax.shard_map(
        functools.partial(local, mesh.shape["gx"], mesh.shape["gy"]),
        mesh=mesh,
        in_specs=(placed,),
        out_specs=(placed,) * 4,
        check_vma=False,
    )
```

```python
import functools
import math

import jax
import jax.numpy as jnp
from jax import lax
from jax.experimental import pallas as pl
from jax.experimental.pallas import tpu as pltpu
from jax.sharding import PartitionSpec as P

FIRST_NEAR = 7.0 / 9.0
FIRST_FAR = 1.0 / 36.0
SECOND_NEAR = 12.0 / 11.0
SECOND_FAR = 3.0 / 44.0
COUPLINGS = (1.0 / 3.0, 2.0 / 11.0)
DIFFERENCES = ((FIRST_NEAR, FIRST_FAR, 1.0), (SECOND_NEAR, SECOND_FAR, -1.0))
MESH = pl.DeviceIdType.MESH
HALO = 24
F32 = jnp.float32


def green(coupling):
    root = math.sqrt(1.0 - 4.0 * coupling * coupling)
    return (1.0 - root) / (2.0 * coupling), 1.0 / root


def powers(coupling, distance):
    ratio, scale = green(coupling)
    size = scale * jnp.exp(distance.astype(F32) * math.log(ratio))
    return jnp.where(distance % 2 == 0, size, -size)


def stencils(u, axis):
    n = u.shape[axis]
    plus_one = pltpu.roll(u, n - 1, axis)
    minus_one = pltpu.roll(u, 1, axis)
    plus_two = pltpu.roll(u, n - 2, axis)
    minus_two = pltpu.roll(u, 2, axis)
    first = FIRST_NEAR * (plus_one - minus_one) + FIRST_FAR * (plus_two - minus_two)
    second = SECOND_NEAR * (plus_one - 2.0 * u + minus_one) + SECOND_FAR * (
        plus_two - 2.0 * u + minus_two
    )
    return first, second


def iota(shape, axis):
    return lax.broadcasted_iota(jnp.int32, shape, axis)


def dot(a, b):
    return jnp.dot(a, b, precision=lax.Precision.HIGHEST, preferred_element_type=F32)


def kernel(
    nx,
    ny,
    v_ref,
    dx_ref,
    dy_ref,
    dxx_ref,
    dyy_ref,
    edge_ref,
    weight_ref,
    u_ref,
    xr,
    yl,
    yr,
    pool,
    recv,
    ready,
):
    pl.run_scoped(
        functools.partial(
            body,
            nx,
            ny,
            v_ref,
            dx_ref,
            dy_ref,
            dxx_ref,
            dyy_ref,
            edge_ref,
            weight_ref,
            u_ref,
            xr,
            yl,
            yr,
            pool,
            recv,
            ready,
        ),
        pltpu.SemaphoreType.DMA,
        pltpu.SemaphoreType.DMA,
    )


def body(
    nx,
    ny,
    v_ref,
    dx_ref,
    dy_ref,
    dxx_ref,
    dyy_ref,
    edge_ref,
    weight_ref,
    u_ref,
    xr,
    yl,
    yr,
    pool,
    recv,
    ready,
    load_sem,
    send,
):
    ix = lax.axis_index("gx")
    iy = lax.axis_index("gy")
    up = {"gx": jnp.where(ix == nx - 1, 0, ix + 1)}
    down = {"gx": jnp.where(ix == 0, nx - 1, ix - 1)}
    right = {"gy": jnp.where(iy == ny - 1, 0, iy + 1)}
    left = {"gy": jnp.where(iy == 0, ny - 1, iy - 1)}
    rows, cols = u_ref.shape
    first = ix == 0
    last = ix == nx - 1
    before = ix == nx - 2
    odd = lax.rem(iy, 2)

    def signal(semaphore, other):
        pl.semaphore_signal(semaphore, inc=1, device_id=other, device_id_type=MESH)

    def remote(k, src, dst, other):
        return pltpu.make_async_remote_copy(
            src_ref=src,
            dst_ref=dst,
            send_sem=send,
            recv_sem=recv.at[k],
            device_id=other,
            device_id_type=MESH,
        )

    def take(count, semaphore):
        part = pool.at[pl.ds(0, count), :]
        pltpu.make_async_copy(part, part, semaphore).wait()

    load = pltpu.make_async_copy(v_ref.at[0], u_ref, load_sem)
    to_up = remote(0, v_ref.at[0, pl.ds(rows - HALO, HALO), :], edge_ref.at[pl.ds(0, HALO), :], up)
    to_down = remote(1, v_ref.at[0, pl.ds(0, HALO), :], xr, down)
    to_right = remote(1, v_ref.at[0, :, pl.ds(cols - 128, 128)], yl, right)
    to_left = remote(1, v_ref.at[0, :, pl.ds(0, 128)], yr, left)

    barrier = pltpu.get_barrier_semaphore()

    def greet_sides():
        signal(barrier, left)
        signal(barrier, right)

    def answer_sides():
        signal(ready.at[0], right)
        signal(ready.at[0], left)

    @pl.when(jnp.logical_not(last))
    def _():
        signal(barrier, down)
        pl.when(jnp.logical_not(before))(lambda: signal(barrier, up))
        pl.when((odd == 1) & jnp.logical_not(before))(greet_sides)
        pl.semaphore_wait(barrier, jnp.where(first, 1, 2) + 2 * (1 - odd))
        to_up.start()

        @pl.when(before)
        def _():
            signal(ready.at[0], up)
            pl.when(odd == 0)(lambda: signal(ready.at[1], up))
            pl.when(odd == 1)(greet_sides)

        pl.when(jnp.logical_not(first))(lambda: to_down.start())
        pl.when(odd == 0)(answer_sides)

        @pl.when(odd == 1)
        def _():
            pl.semaphore_wait(ready.at[0], 2)
            pl.when(before)(lambda: signal(ready.at[1], up))

        to_right.start()
        to_left.start()

    @pl.when(last)
    def _():
        pl.semaphore_wait(barrier, 1)
        to_up.start()
        signal(ready.at[1], up)
        signal(barrier, down)

    load.start()
    distance = jnp.abs(iota((rows, rows), 0) - iota((rows, rows), 1))
    across = [powers(c, distance) for c in COUPLINGS]
    distance = jnp.abs(iota((cols, cols), 0) - iota((cols, cols), 1))
    along = [powers(c, distance) for c in COUPLINGS]
    edge = HALO + 8
    place = iota((edge, cols), 0)
    tail = iota((HALO, cols), 0)
    above = []
    for k, c in enumerate(COUPLINGS):
        _, scale = green(c)
        near, far, side = DIFFERENCES[k]
        sum_weight = 0.0
        row_weight = 0.0
        for shift, factor in ((1, far), (0, near + far), (-1, side * (near + far)), (-2, side * far)):
            at = place - shift
            held = jnp.where((at >= 2) & (at <= HALO), powers(c, jnp.abs(HALO - at)), 0.0) / scale
            sum_weight += factor * held
            row_weight += jnp.where(at == HALO + 1, factor, 0.0)
        weight_ref[k, pl.ds(0, edge), :] = sum_weight
        weight_ref[k, pl.ds(edge + 2 * HALO, edge), :] = row_weight
        weight_ref[k, pl.ds(edge, HALO), :] = powers(c, tail)
        weight_ref[k, pl.ds(edge + HALO, HALO), :] = powers(c, jnp.abs(tail - 1))
        above.append(
            (
                jnp.where((place >= 7) & (place < edge - 2), powers(c, jnp.abs(place - 7)), 0.0) / scale,
                powers(c, HALO - 1 - tail),
                powers(c, jnp.abs(HALO - 2 - tail)),
            )
        )
    lane = iota((rows, 128), 1)
    source = iota((128, 128), 0)
    target = iota((128, 128), 1)
    sides = [[powers(c, jnp.abs(target - source + shift)) for c in COUPLINGS] for shift in (64, -64)]

    load.wait()
    u = u_ref[...]
    edge_ref[pl.ds(HALO, 8), :] = u[:8]
    near = [pltpu.roll(u[:, :128], 64, 1), pltpu.roll(u[:, cols - 128 :], 64, 1)]

    row = iota((rows, cols), 0)
    col = iota((rows, cols), 1)
    inner = (row >= 2) & (row < rows - 2)
    for out, g, s in zip((dx_ref, dxx_ref), across, stencils(u, 0)):
        out[0] = dot(g, jnp.where(inner, s, 0.0))
    inner = (col >= 2) & (col < cols - 2)
    fy = [dot(jnp.where(inner, s, 0.0), g) for g, s in zip(along, stencils(u, 1))]

    @pl.when(last)
    def _():
        pl.semaphore_wait(ready.at[0], 1)
        to_down.start()
        pl.semaphore_wait(ready.at[1], 1)
        to_right.start()
        to_left.start()

    @pl.when(first)
    def _():
        pl.semaphore_wait(ready.at[1], 1)
        remote(1, u_ref.at[pl.ds(0, HALO), :], xr, down).start()

    take(rows + HALO, recv.at[1])
    lower = stencils(jnp.where(lane < 64, pltpu.roll(yl[...], 64, 1), near[0]), 1)
    upper = stencils(jnp.where(lane < 64, near[1], pltpu.roll(yr[...], 64, 1)), 1)
    for k, out in enumerate((dy_ref, dyy_ref)):
        low = jnp.where((lane >= 2) & (lane < 66), lower[k], 0.0)
        high = jnp.where((lane >= 62) & (lane < 126), upper[k], 0.0)
        out[0] = fy[k] + jnp.concatenate(
            [dot(low, sides[0][k]), dot(high, sides[1][k])], axis=1
        )

    upper = stencils(jnp.concatenate([u[rows - 8 :], xr[...]], axis=0), 0)
    for k, out in enumerate((dx_ref, dxx_ref)):
        weight, far, close = above[k]
        total = jnp.sum(weight * upper[k], axis=0, keepdims=True)
        out[0, pl.ds(rows - HALO, HALO), :] += far * total + close * upper[k][6:7]

    take(rows + 2 * HALO, send)
    to_up.wait_recv()


def finish(
    dx_in, dy_in, dxx_in, dyy_in, edge_ref, weight_ref, dx_ref, dy_ref, dxx_ref, dyy_ref, low, pool, sem
):
    rest = pl.ds(HALO, dx_in.shape[1] - HALO)
    copies = [
        pltpu.make_async_copy(dy_in, dy_ref, sem),
        pltpu.make_async_copy(dyy_in, dyy_ref, sem),
        pltpu.make_async_copy(dx_in.at[0, rest, :], dx_ref.at[0, rest, :], sem),
        pltpu.make_async_copy(dxx_in.at[0, rest, :], dxx_ref.at[0, rest, :], sem),
    ]
    for copy in copies:
        copy.start()
    edge = HALO + 8
    head = pl.ds(0, HALO)
    held = edge_ref[...]
    steps = pltpu.roll(held, edge - 1, 0) - held
    for k, (part, out) in enumerate(((dx_in, dx_ref), (dxx_in, dxx_ref))):
        total = jnp.sum(weight_ref[k, pl.ds(0, edge), :] * steps, axis=0, keepdims=True)
        source = jnp.sum(
            weight_ref[k, pl.ds(edge + 3 * HALO - 8, 16), :] * steps[HALO - 8 : HALO + 8],
            axis=0,
            keepdims=True,
        )
        low[k] = (
            part[0, head, :]
            + weight_ref[k, pl.ds(edge, HALO), :] * total
            + weight_ref[k, pl.ds(edge + HALO, HALO), :] * source
        )
        pltpu.make_async_copy(low.at[k], out.at[0, head, :], sem).start()
    pltpu.make_async_copy(pool, pool, sem).wait()


def local(nx, ny, velocity):
    _, rows, cols = velocity.shape
    out = jax.ShapeDtypeStruct(velocity.shape, F32)
    vmem = pl.BlockSpec(memory_space=pltpu.VMEM)
    anywhere = pl.BlockSpec(memory_space=pl.ANY)
    fields = pl.pallas_call(
        functools.partial(kernel, nx, ny),
        out_shape=(pltpu.VMEM(velocity.shape, F32),) * 4
        + (pltpu.VMEM((HALO + 8, cols), F32), pltpu.VMEM((2, 4 * HALO + 16, cols), F32)),
        in_specs=[anywhere],
        out_specs=[vmem] * 6,
        scratch_shapes=[
            pltpu.VMEM((rows, cols), F32),
            pltpu.VMEM((HALO, cols), F32),
            pltpu.VMEM((rows, 128), F32),
            pltpu.VMEM((rows, 128), F32),
            pltpu.VMEM((rows + 2 * HALO, cols), F32),
            pltpu.SemaphoreType.DMA((2,)),
            pltpu.SemaphoreType.REGULAR((2,)),
        ],
        compiler_params=pltpu.CompilerParams(collective_id=0, has_side_effects=True),
    )(velocity)
    return pl.pallas_call(
        finish,
        out_shape=(out,) * 4,
        in_specs=[vmem] * 6,
        out_specs=[anywhere] * 4,
        scratch_shapes=[
            pltpu.VMEM((2, HALO, cols), F32),
            pltpu.VMEM((4 * rows, cols), F32),
            pltpu.SemaphoreType.DMA,
        ],
    )(*[pltpu.with_memory_space_constraint(f, pltpu.VMEM) for f in fields])


def solution(mesh):
    placed = P(None, "gx", "gy")
    return jax.shard_map(
        functools.partial(local, mesh.shape["gx"], mesh.shape["gy"]),
        mesh=mesh,
        in_specs=(placed,),
        out_specs=(placed,) * 4,
        check_vma=False,
    )
```

```python
import functools
import math

import jax
import jax.numpy as jnp
from jax import lax
from jax.experimental import pallas as pl
from jax.experimental.pallas import tpu as pltpu
from jax.sharding import PartitionSpec as P

FIRST_NEAR = 7.0 / 9.0
FIRST_FAR = 1.0 / 36.0
SECOND_NEAR = 12.0 / 11.0
SECOND_FAR = 3.0 / 44.0
COUPLINGS = (1.0 / 3.0, 2.0 / 11.0)
DIFFERENCES = ((FIRST_NEAR, FIRST_FAR, 1.0), (SECOND_NEAR, SECOND_FAR, -1.0))
MESH = pl.DeviceIdType.MESH
HALO = 24
F32 = jnp.float32


def green(coupling):
    root = math.sqrt(1.0 - 4.0 * coupling * coupling)
    return (1.0 - root) / (2.0 * coupling), 1.0 / root


def powers(coupling, distance):
    ratio, scale = green(coupling)
    size = scale * jnp.exp(distance.astype(F32) * math.log(ratio))
    return jnp.where(distance % 2 == 0, size, -size)


def stencils(u, axis):
    n = u.shape[axis]
    plus_one = pltpu.roll(u, n - 1, axis)
    minus_one = pltpu.roll(u, 1, axis)
    plus_two = pltpu.roll(u, n - 2, axis)
    minus_two = pltpu.roll(u, 2, axis)
    first = FIRST_NEAR * (plus_one - minus_one) + FIRST_FAR * (plus_two - minus_two)
    second = SECOND_NEAR * (plus_one - 2.0 * u + minus_one) + SECOND_FAR * (
        plus_two - 2.0 * u + minus_two
    )
    return first, second


def iota(shape, axis):
    return lax.broadcasted_iota(jnp.int32, shape, axis)


def dot(a, b):
    return jnp.dot(a, b, precision=lax.Precision.HIGHEST, preferred_element_type=F32)


def kernel(
    nx,
    ny,
    v_ref,
    dx_ref,
    dy_ref,
    dxx_ref,
    dyy_ref,
    edge_ref,
    weight_ref,
    u_ref,
    xr,
    yl,
    yr,
    pool,
    recv,
    ready,
):
    pl.run_scoped(
        functools.partial(
            body,
            nx,
            ny,
            v_ref,
            dx_ref,
            dy_ref,
            dxx_ref,
            dyy_ref,
            edge_ref,
            weight_ref,
            u_ref,
            xr,
            yl,
            yr,
            pool,
            recv,
            ready,
        ),
        pltpu.SemaphoreType.DMA,
        pltpu.SemaphoreType.DMA,
    )


def body(
    nx,
    ny,
    v_ref,
    dx_ref,
    dy_ref,
    dxx_ref,
    dyy_ref,
    edge_ref,
    weight_ref,
    u_ref,
    xr,
    yl,
    yr,
    pool,
    recv,
    ready,
    load_sem,
    send,
):
    ix = lax.axis_index("gx")
    iy = lax.axis_index("gy")
    up = {"gx": jnp.where(ix == nx - 1, 0, ix + 1)}
    down = {"gx": jnp.where(ix == 0, nx - 1, ix - 1)}
    right = {"gy": jnp.where(iy == ny - 1, 0, iy + 1)}
    left = {"gy": jnp.where(iy == 0, ny - 1, iy - 1)}
    rows, cols = u_ref.shape
    first = ix == 0
    last = ix == nx - 1
    before = ix == nx - 2
    odd = jnp.bitwise_and(iy, 1)

    def signal(semaphore, other):
        pl.semaphore_signal(semaphore, inc=1, device_id=other, device_id_type=MESH)

    def remote(k, src, dst, other):
        return pltpu.make_async_remote_copy(
            src_ref=src,
            dst_ref=dst,
            send_sem=send,
            recv_sem=recv.at[k],
            device_id=other,
            device_id_type=MESH,
        )

    def take(count, semaphore):
        part = pool.at[pl.ds(0, count), :]
        pltpu.make_async_copy(part, part, semaphore).wait()

    load = pltpu.make_async_copy(v_ref.at[0], u_ref, load_sem)
    to_up = remote(0, v_ref.at[0, pl.ds(rows - HALO, HALO), :], edge_ref.at[pl.ds(0, HALO), :], up)
    to_down = remote(1, v_ref.at[0, pl.ds(0, HALO), :], xr, down)
    to_right = remote(1, v_ref.at[0, :, pl.ds(cols - 128, 128)], yl, right)
    to_left = remote(1, v_ref.at[0, :, pl.ds(0, 128)], yr, left)

    barrier = pltpu.get_barrier_semaphore()

    def greet_sides():
        signal(barrier, left)
        signal(barrier, right)

    def answer_sides():
        signal(ready.at[0], right)
        signal(ready.at[0], left)

    @pl.when(jnp.logical_not(last))
    def _():
        signal(barrier, down)
        pl.when(jnp.logical_not(before))(lambda: signal(barrier, up))
        pl.when((odd == 1) & jnp.logical_not(before))(greet_sides)
        pl.semaphore_wait(barrier, jnp.where(first, 1, 2) + 2 * (1 - odd))
        to_up.start()

        @pl.when(before)
        def _():
            signal(ready.at[0], up)
            pl.when(odd == 0)(lambda: signal(ready.at[1], up))
            pl.when(odd == 1)(greet_sides)

        pl.when(jnp.logical_not(first))(lambda: to_down.start())
        pl.when(odd == 0)(answer_sides)

        @pl.when(odd == 1)
        def _():
            pl.semaphore_wait(ready.at[0], 2)
            pl.when(before)(lambda: signal(ready.at[1], up))

        to_right.start()
        to_left.start()

    @pl.when(last)
    def _():
        pl.semaphore_wait(barrier, 1)
        remote(
            0,
            v_ref.at[0, pl.ds(rows - HALO, HALO), :],
            edge_ref.at[pl.ds(0, HALO), :],
            {"gx": 0},
        ).start()
        signal(ready.at[1], {"gx": 0})
        signal(barrier, down)

    load.start()
    distance = jnp.abs(iota((rows, rows), 0) - iota((rows, rows), 1))
    across = [powers(c, distance) for c in COUPLINGS]
    distance = jnp.abs(iota((cols, cols), 0) - iota((cols, cols), 1))
    along = [powers(c, distance) for c in COUPLINGS]
    edge = HALO + 8
    place = iota((edge, cols), 0)
    tail = iota((HALO, cols), 0)
    above = []
    for k, c in enumerate(COUPLINGS):
        _, scale = green(c)
        near, far, side = DIFFERENCES[k]
        sum_weight = 0.0
        row_weight = 0.0
        for shift, factor in ((1, far), (0, near + far), (-1, side * (near + far)), (-2, side * far)):
            at = place - shift
            held = jnp.where((at >= 2) & (at <= HALO), powers(c, jnp.abs(HALO - at)), 0.0) / scale
            sum_weight += factor * held
            row_weight += jnp.where(at == HALO + 1, factor, 0.0)
        weight_ref[k, pl.ds(0, edge), :] = sum_weight
        weight_ref[k, pl.ds(edge + 2 * HALO, edge), :] = row_weight
        weight_ref[k, pl.ds(edge, HALO), :] = powers(c, tail)
        weight_ref[k, pl.ds(edge + HALO, HALO), :] = powers(c, jnp.abs(tail - 1))
        above.append(
            (
                jnp.where((place >= 7) & (place < edge - 2), powers(c, jnp.abs(place - 7)), 0.0) / scale,
                powers(c, HALO - 1 - tail),
                powers(c, jnp.abs(HALO - 2 - tail)),
            )
        )
    lane = iota((rows, 128), 1)
    source = iota((128, 128), 0)
    target = iota((128, 128), 1)
    sides = [[powers(c, jnp.abs(target - source + shift)) for c in COUPLINGS] for shift in (64, -64)]

    load.wait()
    u = u_ref[...]
    edge_ref[pl.ds(HALO, 8), :] = u[:8]
    near = [pltpu.roll(u[:, :128], 64, 1), pltpu.roll(u[:, cols - 128 :], 64, 1)]

    row = iota((rows, cols), 0)
    col = iota((rows, cols), 1)
    inner = (row >= 2) & (row < rows - 2)
    for out, g, s in zip((dx_ref, dxx_ref), across, stencils(u, 0)):
        out[0] = dot(g, jnp.where(inner, s, 0.0))
    inner = (col >= 2) & (col < cols - 2)
    fy = [dot(jnp.where(inner, s, 0.0), g) for g, s in zip(along, stencils(u, 1))]

    @pl.when(last)
    def _():
        pl.semaphore_wait(ready.at[0], 1)
        to_down.start()
        pl.semaphore_wait(ready.at[1], 1)
        to_right.start()
        to_left.start()

    @pl.when(first)
    def _():
        pl.semaphore_wait(ready.at[1], 1)
        remote(1, u_ref.at[pl.ds(0, HALO), :], xr, down).start()

    take(rows + HALO, recv.at[1])
    lower = stencils(jnp.where(lane < 64, pltpu.roll(yl[...], 64, 1), near[0]), 1)
    upper = stencils(jnp.where(lane < 64, near[1], pltpu.roll(yr[...], 64, 1)), 1)
    for k, out in enumerate((dy_ref, dyy_ref)):
        low = jnp.where((lane >= 2) & (lane < 66), lower[k], 0.0)
        high = jnp.where((lane >= 62) & (lane < 126), upper[k], 0.0)
        out[0] = fy[k] + jnp.concatenate(
            [dot(low, sides[0][k]), dot(high, sides[1][k])], axis=1
        )

    upper = stencils(jnp.concatenate([u[rows - 8 :], xr[...]], axis=0), 0)
    for k, out in enumerate((dx_ref, dxx_ref)):
        weight, far, close = above[k]
        total = jnp.sum(weight * upper[k], axis=0, keepdims=True)
        out[0, pl.ds(rows - HALO, HALO), :] += far * total + close * upper[k][6:7]

    take(rows + 2 * HALO, send)
    to_up.wait_recv()


def finish(
    dx_in, dy_in, dxx_in, dyy_in, edge_ref, weight_ref, dx_ref, dy_ref, dxx_ref, dyy_ref, low, pool, sem
):
    rest = pl.ds(HALO, dx_in.shape[1] - HALO)
    copies = [
        pltpu.make_async_copy(dy_in, dy_ref, sem),
        pltpu.make_async_copy(dyy_in, dyy_ref, sem),
        pltpu.make_async_copy(dx_in.at[0, rest, :], dx_ref.at[0, rest, :], sem),
        pltpu.make_async_copy(dxx_in.at[0, rest, :], dxx_ref.at[0, rest, :], sem),
    ]
    for copy in copies:
        copy.start()
    edge = HALO + 8
    head = pl.ds(0, HALO)
    held = edge_ref[...]
    steps = pltpu.roll(held, edge - 1, 0) - held
    for k, (part, out) in enumerate(((dx_in, dx_ref), (dxx_in, dxx_ref))):
        total = jnp.sum(weight_ref[k, pl.ds(0, edge), :] * steps, axis=0, keepdims=True)
        source = jnp.sum(
            weight_ref[k, pl.ds(edge + 3 * HALO - 8, 16), :] * steps[HALO - 8 : HALO + 8],
            axis=0,
            keepdims=True,
        )
        low[k] = (
            part[0, head, :]
            + weight_ref[k, pl.ds(edge, HALO), :] * total
            + weight_ref[k, pl.ds(edge + HALO, HALO), :] * source
        )
        pltpu.make_async_copy(low.at[k], out.at[0, head, :], sem).start()
    pltpu.make_async_copy(pool, pool, sem).wait()


def local(nx, ny, velocity):
    _, rows, cols = velocity.shape
    out = jax.ShapeDtypeStruct(velocity.shape, F32)
    vmem = pl.BlockSpec(memory_space=pltpu.VMEM)
    anywhere = pl.BlockSpec(memory_space=pl.ANY)
    fields = pl.pallas_call(
        functools.partial(kernel, nx, ny),
        out_shape=(pltpu.VMEM(velocity.shape, F32),) * 4
        + (pltpu.VMEM((HALO + 8, cols), F32), pltpu.VMEM((2, 4 * HALO + 16, cols), F32)),
        in_specs=[anywhere],
        out_specs=[vmem] * 6,
        scratch_shapes=[
            pltpu.VMEM((rows, cols), F32),
            pltpu.VMEM((HALO, cols), F32),
            pltpu.VMEM((rows, 128), F32),
            pltpu.VMEM((rows, 128), F32),
            pltpu.VMEM((rows + 2 * HALO, cols), F32),
            pltpu.SemaphoreType.DMA((2,)),
            pltpu.SemaphoreType.REGULAR((2,)),
        ],
        compiler_params=pltpu.CompilerParams(collective_id=0, has_side_effects=True),
    )(velocity)
    return pl.pallas_call(
        finish,
        out_shape=(out,) * 4,
        in_specs=[vmem] * 6,
        out_specs=[anywhere] * 4,
        scratch_shapes=[
            pltpu.VMEM((2, HALO, cols), F32),
            pltpu.VMEM((4 * rows, cols), F32),
            pltpu.SemaphoreType.DMA,
        ],
    )(*[pltpu.with_memory_space_constraint(f, pltpu.VMEM) for f in fields])


def solution(mesh):
    placed = P(None, "gx", "gy")
    return jax.shard_map(
        functools.partial(local, mesh.shape["gx"], mesh.shape["gy"]),
        mesh=mesh,
        in_specs=(placed,),
        out_specs=(placed,) * 4,
        check_vma=False,
    )
```

```python
import functools
import math

import jax
import jax.numpy as jnp
from jax import lax
from jax.experimental import pallas as pl
from jax.experimental.pallas import tpu as pltpu
from jax.sharding import PartitionSpec as P

FIRST_NEAR = 7.0 / 9.0
FIRST_FAR = 1.0 / 36.0
SECOND_NEAR = 12.0 / 11.0
SECOND_FAR = 3.0 / 44.0
COUPLINGS = (1.0 / 3.0, 2.0 / 11.0)
DIFFERENCES = ((FIRST_NEAR, FIRST_FAR, 1.0), (SECOND_NEAR, SECOND_FAR, -1.0))
MESH = pl.DeviceIdType.MESH
HALO = 24
F32 = jnp.float32


def green(coupling):
    root = math.sqrt(1.0 - 4.0 * coupling * coupling)
    return (1.0 - root) / (2.0 * coupling), 1.0 / root


def powers(coupling, distance):
    ratio, scale = green(coupling)
    size = scale * jnp.exp(distance.astype(F32) * math.log(ratio))
    return jnp.where(distance % 2 == 0, size, -size)


def stencils(u, axis):
    n = u.shape[axis]
    plus_one = pltpu.roll(u, n - 1, axis)
    minus_one = pltpu.roll(u, 1, axis)
    plus_two = pltpu.roll(u, n - 2, axis)
    minus_two = pltpu.roll(u, 2, axis)
    first = FIRST_NEAR * (plus_one - minus_one) + FIRST_FAR * (plus_two - minus_two)
    second = SECOND_NEAR * (plus_one - 2.0 * u + minus_one) + SECOND_FAR * (
        plus_two - 2.0 * u + minus_two
    )
    return first, second


def iota(shape, axis):
    return lax.broadcasted_iota(jnp.int32, shape, axis)


def dot(a, b):
    return jnp.dot(a, b, precision=lax.Precision.HIGHEST, preferred_element_type=F32)


def kernel(
    nx,
    ny,
    v_ref,
    dx_ref,
    dy_ref,
    dxx_ref,
    dyy_ref,
    edge_ref,
    weight_ref,
    u_ref,
    xr,
    yl,
    yr,
    pool,
    recv,
    ready,
):
    pl.run_scoped(
        functools.partial(
            body,
            nx,
            ny,
            v_ref,
            dx_ref,
            dy_ref,
            dxx_ref,
            dyy_ref,
            edge_ref,
            weight_ref,
            u_ref,
            xr,
            yl,
            yr,
            pool,
            recv,
            ready,
        ),
        pltpu.SemaphoreType.DMA,
        pltpu.SemaphoreType.DMA,
    )


def body(
    nx,
    ny,
    v_ref,
    dx_ref,
    dy_ref,
    dxx_ref,
    dyy_ref,
    edge_ref,
    weight_ref,
    u_ref,
    xr,
    yl,
    yr,
    pool,
    recv,
    ready,
    load_sem,
    send,
):
    ix = lax.axis_index("gx")
    iy = lax.axis_index("gy")
    up = {"gx": jnp.where(ix == nx - 1, 0, ix + 1)}
    down = {"gx": jnp.where(ix == 0, nx - 1, ix - 1)}
    right = {"gy": jnp.where(iy == ny - 1, 0, iy + 1)}
    left = {"gy": jnp.where(iy == 0, ny - 1, iy - 1)}
    rows, cols = u_ref.shape
    first = ix == 0
    last = ix == nx - 1
    before = ix == nx - 2
    odd = lax.rem(iy, 2)

    def signal(semaphore, other):
        pl.semaphore_signal(semaphore, inc=1, device_id=other, device_id_type=MESH)

    def remote(k, src, dst, other):
        return pltpu.make_async_remote_copy(
            src_ref=src,
            dst_ref=dst,
            send_sem=send,
            recv_sem=recv.at[k],
            device_id=other,
            device_id_type=MESH,
        )

    def take(count, semaphore):
        part = pool.at[pl.ds(0, count), :]
        pltpu.make_async_copy(part, part, semaphore).wait()

    load = pltpu.make_async_copy(v_ref.at[0], u_ref, load_sem)
    to_up = remote(0, v_ref.at[0, pl.ds(rows - HALO, HALO), :], edge_ref.at[pl.ds(0, HALO), :], up)
    to_down = remote(1, v_ref.at[0, pl.ds(0, HALO), :], xr, down)
    to_right = remote(1, v_ref.at[0, :, pl.ds(cols - 128, 128)], yl, right)
    to_left = remote(1, v_ref.at[0, :, pl.ds(0, 128)], yr, left)

    barrier = pltpu.get_barrier_semaphore()

    def greet_sides():
        signal(barrier, left)
        signal(barrier, right)

    def answer_sides():
        signal(ready.at[0], right)
        signal(ready.at[0], left)

    @pl.when(jnp.logical_not(last))
    def _():
        signal(barrier, down)
        pl.when(jnp.logical_not(before))(lambda: signal(barrier, up))
        pl.when((odd == 1) & jnp.logical_not(before))(greet_sides)
        pl.semaphore_wait(barrier, jnp.where(first, 1, 2) + 2 * (1 - odd))
        to_up.start()

        @pl.when(before)
        def _():
            signal(ready.at[0], up)
            pl.when(odd == 0)(lambda: signal(ready.at[1], up))
            pl.when(odd == 1)(greet_sides)

        pl.when(jnp.logical_not(first))(lambda: to_down.start())
        pl.when(odd == 0)(answer_sides)

        @pl.when(odd == 1)
        def _():
            pl.semaphore_wait(ready.at[0], 2)
            pl.when(before)(lambda: signal(ready.at[1], up))

        to_right.start()
        to_left.start()

    @pl.when(last)
    def _():
        pl.semaphore_wait(barrier, 1)
        to_up.start()
        signal(ready.at[1], up)
        signal(barrier, down)

    load.start()
    distance = jnp.abs(iota((rows, rows), 0) - iota((rows, rows), 1))
    across = [powers(c, distance) for c in COUPLINGS]
    distance = jnp.abs(iota((cols, cols), 0) - iota((cols, cols), 1))
    along = [powers(c, distance) for c in COUPLINGS]
    edge = HALO + 8
    place = iota((edge, cols), 0)
    tail = iota((HALO, cols), 0)
    above = []
    for k, c in enumerate(COUPLINGS):
        _, scale = green(c)
        near, far, side = DIFFERENCES[k]
        sum_weight = 0.0
        row_weight = 0.0
        for shift, factor in ((1, far), (0, near + far), (-1, side * (near + far)), (-2, side * far)):
            at = place - shift
            held = jnp.where((at >= 2) & (at <= HALO), powers(c, jnp.abs(HALO - at)), 0.0) / scale
            sum_weight += factor * held
            row_weight += jnp.where(at == HALO + 1, factor, 0.0)
        weight_ref[k, pl.ds(0, edge), :] = sum_weight
        weight_ref[k, pl.ds(edge + 2 * HALO, edge), :] = row_weight
        weight_ref[k, pl.ds(edge, HALO), :] = powers(c, tail)
        weight_ref[k, pl.ds(edge + HALO, HALO), :] = powers(c, jnp.abs(tail - 1))
        above.append(
            (
                jnp.where((place >= 7) & (place < edge - 2), powers(c, jnp.abs(place - 7)), 0.0) / scale,
                powers(c, HALO - 1 - tail),
                powers(c, jnp.abs(HALO - 2 - tail)),
            )
        )
    lane = iota((rows, 128), 1)
    source = iota((128, 128), 0)
    target = iota((128, 128), 1)
    sides = [[powers(c, jnp.abs(target - source + shift)) for c in COUPLINGS] for shift in (64, -64)]

    load.wait()
    u = u_ref[...]
    edge_ref[pl.ds(HALO, 8), :] = u[:8]
    near = [pltpu.roll(u[:, :128], 64, 1), pltpu.roll(u[:, cols - 128 :], 64, 1)]

    row = iota((rows, cols), 0)
    col = iota((rows, cols), 1)
    inner = (row >= 2) & (row < rows - 2)
    for out, g, s in zip((dx_ref, dxx_ref), across, stencils(u, 0)):
        out[0] = dot(g, jnp.where(inner, s, 0.0))
    inner = (col >= 2) & (col < cols - 2)
    fy = [dot(jnp.where(inner, s, 0.0), g) for g, s in zip(along, stencils(u, 1))]

    @pl.when(last)
    def _():
        pl.semaphore_wait(ready.at[0], 1)
        to_down.start()
        pl.semaphore_wait(ready.at[1], 1)
        to_right.start()
        to_left.start()

    @pl.when(first)
    def _():
        pl.semaphore_wait(ready.at[1], 1)
        remote(1, u_ref.at[pl.ds(0, HALO), :], xr, down).start()

    take(rows + HALO, recv.at[1])
    lower = stencils(jnp.where(lane < 64, pltpu.roll(yl[...], 64, 1), near[0]), 1)
    upper = stencils(jnp.where(lane < 64, near[1], pltpu.roll(yr[...], 64, 1)), 1)
    for k, out in enumerate((dy_ref, dyy_ref)):
        low = jnp.where((lane >= 2) & (lane < 66), lower[k], 0.0)
        high = jnp.where((lane >= 62) & (lane < 126), upper[k], 0.0)
        out[0] = fy[k] + jnp.concatenate(
            [dot(low, sides[0][k]), dot(high, sides[1][k])], axis=1
        )

    upper = stencils(jnp.concatenate([u[rows - 8 :], xr[...]], axis=0), 0)
    for k, out in enumerate((dx_ref, dxx_ref)):
        weight, far, close = above[k]
        total = jnp.sum(weight * upper[k], axis=0, keepdims=True)
        out[0, pl.ds(rows - HALO, HALO), :] += far * total + close * upper[k][6:7]

    take(rows + 2 * HALO, send)
    to_up.wait_recv()


def finish(
    dx_in, dy_in, dxx_in, dyy_in, edge_ref, weight_ref, dx_ref, dy_ref, dxx_ref, dyy_ref, low, pool, sem
):
    rest = pl.ds(HALO, dx_in.shape[1] - HALO)
    half = pl.ds(0, dx_in.shape[1] // 2)
    other = pl.ds(dx_in.shape[1] // 2, dx_in.shape[1] // 2)
    for part, out, place in (
        (dy_in, dy_ref, half),
        (dyy_in, dyy_ref, half),
        (dx_in, dx_ref, rest),
        (dxx_in, dxx_ref, rest),
        (dy_in, dy_ref, other),
        (dyy_in, dyy_ref, other),
    ):
        pltpu.make_async_copy(part.at[0, place, :], out.at[0, place, :], sem).start()
    edge = HALO + 8
    head = pl.ds(0, HALO)
    held = edge_ref[...]
    steps = pltpu.roll(held, edge - 1, 0) - held
    for k, (part, out) in enumerate(((dx_in, dx_ref), (dxx_in, dxx_ref))):
        total = jnp.sum(weight_ref[k, pl.ds(0, edge), :] * steps, axis=0, keepdims=True)
        source = jnp.sum(
            weight_ref[k, pl.ds(edge + 3 * HALO - 8, 16), :] * steps[HALO - 8 : HALO + 8],
            axis=0,
            keepdims=True,
        )
        low[k] = (
            part[0, head, :]
            + weight_ref[k, pl.ds(edge, HALO), :] * total
            + weight_ref[k, pl.ds(edge + HALO, HALO), :] * source
        )
        pltpu.make_async_copy(low.at[k], out.at[0, head, :], sem).start()
    pltpu.make_async_copy(pool, pool, sem).wait()


def local(nx, ny, velocity):
    _, rows, cols = velocity.shape
    out = jax.ShapeDtypeStruct(velocity.shape, F32)
    vmem = pl.BlockSpec(memory_space=pltpu.VMEM)
    anywhere = pl.BlockSpec(memory_space=pl.ANY)
    fields = pl.pallas_call(
        functools.partial(kernel, nx, ny),
        out_shape=(pltpu.VMEM(velocity.shape, F32),) * 4
        + (pltpu.VMEM((HALO + 8, cols), F32), pltpu.VMEM((2, 4 * HALO + 16, cols), F32)),
        in_specs=[anywhere],
        out_specs=[vmem] * 6,
        scratch_shapes=[
            pltpu.VMEM((rows, cols), F32),
            pltpu.VMEM((HALO, cols), F32),
            pltpu.VMEM((rows, 128), F32),
            pltpu.VMEM((rows, 128), F32),
            pltpu.VMEM((rows + 2 * HALO, cols), F32),
            pltpu.SemaphoreType.DMA((2,)),
            pltpu.SemaphoreType.REGULAR((2,)),
        ],
        compiler_params=pltpu.CompilerParams(collective_id=0, has_side_effects=True),
    )(velocity)
    return pl.pallas_call(
        finish,
        out_shape=(out,) * 4,
        in_specs=[vmem] * 6,
        out_specs=[anywhere] * 4,
        scratch_shapes=[
            pltpu.VMEM((2, HALO, cols), F32),
            pltpu.VMEM((4 * rows, cols), F32),
            pltpu.SemaphoreType.DMA,
        ],
    )(*[pltpu.with_memory_space_constraint(f, pltpu.VMEM) for f in fields])


def solution(mesh):
    placed = P(None, "gx", "gy")
    return jax.shard_map(
        functools.partial(local, mesh.shape["gx"], mesh.shape["gy"]),
        mesh=mesh,
        in_specs=(placed,),
        out_specs=(placed,) * 4,
        check_vma=False,
    )
```

```python
import functools
import math

import jax
import jax.numpy as jnp
from jax import lax
from jax.experimental import pallas as pl
from jax.experimental.pallas import tpu as pltpu
from jax.sharding import PartitionSpec as P

FIRST_NEAR = 7.0 / 9.0
FIRST_FAR = 1.0 / 36.0
SECOND_NEAR = 12.0 / 11.0
SECOND_FAR = 3.0 / 44.0
COUPLINGS = (1.0 / 3.0, 2.0 / 11.0)
DIFFERENCES = ((FIRST_NEAR, FIRST_FAR, 1.0), (SECOND_NEAR, SECOND_FAR, -1.0))
MESH = pl.DeviceIdType.MESH
HALO = 24
F32 = jnp.float32


def green(coupling):
    root = math.sqrt(1.0 - 4.0 * coupling * coupling)
    return (1.0 - root) / (2.0 * coupling), 1.0 / root


def powers(coupling, distance):
    ratio, scale = green(coupling)
    size = scale * jnp.exp(distance.astype(F32) * math.log(ratio))
    return jnp.where(distance % 2 == 0, size, -size)


def stencils(u, axis):
    n = u.shape[axis]
    plus_one = pltpu.roll(u, n - 1, axis)
    minus_one = pltpu.roll(u, 1, axis)
    plus_two = pltpu.roll(u, n - 2, axis)
    minus_two = pltpu.roll(u, 2, axis)
    first = FIRST_NEAR * (plus_one - minus_one) + FIRST_FAR * (plus_two - minus_two)
    second = SECOND_NEAR * (plus_one - 2.0 * u + minus_one) + SECOND_FAR * (
        plus_two - 2.0 * u + minus_two
    )
    return first, second


def iota(shape, axis):
    return lax.broadcasted_iota(jnp.int32, shape, axis)


def dot(a, b):
    return jnp.dot(a, b, precision=lax.Precision.HIGHEST, preferred_element_type=F32)


def kernel(
    nx,
    ny,
    v_ref,
    dx_ref,
    dy_ref,
    dxx_ref,
    dyy_ref,
    edge_ref,
    weight_ref,
    u_ref,
    xr,
    yl,
    yr,
    pool,
    recv,
    ready,
):
    pl.run_scoped(
        functools.partial(
            body,
            nx,
            ny,
            v_ref,
            dx_ref,
            dy_ref,
            dxx_ref,
            dyy_ref,
            edge_ref,
            weight_ref,
            u_ref,
            xr,
            yl,
            yr,
            pool,
            recv,
            ready,
        ),
        pltpu.SemaphoreType.DMA,
        pltpu.SemaphoreType.DMA,
    )


def body(
    nx,
    ny,
    v_ref,
    dx_ref,
    dy_ref,
    dxx_ref,
    dyy_ref,
    edge_ref,
    weight_ref,
    u_ref,
    xr,
    yl,
    yr,
    pool,
    recv,
    ready,
    load_sem,
    send,
):
    ix = lax.axis_index("gx")
    iy = lax.axis_index("gy")
    up = {"gx": jnp.where(ix == nx - 1, 0, ix + 1)}
    down = {"gx": jnp.where(ix == 0, nx - 1, ix - 1)}
    right = {"gy": jnp.where(iy == ny - 1, 0, iy + 1)}
    left = {"gy": jnp.where(iy == 0, ny - 1, iy - 1)}
    rows, cols = u_ref.shape
    first = ix == 0
    last = ix == nx - 1
    before = ix == nx - 2
    odd = jnp.bitwise_and(iy, 1)

    def signal(semaphore, other):
        pl.semaphore_signal(semaphore, inc=1, device_id=other, device_id_type=MESH)

    def remote(k, src, dst, other):
        return pltpu.make_async_remote_copy(
            src_ref=src,
            dst_ref=dst,
            send_sem=send,
            recv_sem=recv.at[k],
            device_id=other,
            device_id_type=MESH,
        )

    def take(count, semaphore):
        part = pool.at[pl.ds(0, count), :]
        pltpu.make_async_copy(part, part, semaphore).wait()

    load = pltpu.make_async_copy(v_ref.at[0], u_ref, load_sem)
    to_up = remote(0, v_ref.at[0, pl.ds(rows - HALO, HALO), :], edge_ref.at[pl.ds(0, HALO), :], up)
    to_down = remote(1, v_ref.at[0, pl.ds(0, HALO), :], xr, down)
    to_right = remote(1, v_ref.at[0, :, pl.ds(cols - 128, 128)], yl, right)
    to_left = remote(1, v_ref.at[0, :, pl.ds(0, 128)], yr, left)

    barrier = pltpu.get_barrier_semaphore()

    def greet_sides():
        signal(barrier, left)
        signal(barrier, right)

    def answer_sides():
        signal(ready.at[0], right)
        signal(ready.at[0], left)

    @pl.when(jnp.logical_not(last))
    def _():
        signal(barrier, down)
        pl.when(jnp.logical_not(before))(lambda: signal(barrier, up))
        pl.when((odd == 1) & jnp.logical_not(before))(greet_sides)
        pl.semaphore_wait(barrier, jnp.where(first, 1, 2) + 2 * (1 - odd))
        to_up.start()

        @pl.when(before)
        def _():
            signal(ready.at[0], up)
            pl.when(odd == 0)(lambda: signal(ready.at[1], up))
            pl.when(odd == 1)(greet_sides)

        pl.when(jnp.logical_not(first))(lambda: to_down.start())
        pl.when(odd == 0)(answer_sides)

        @pl.when(odd == 1)
        def _():
            pl.semaphore_wait(ready.at[0], 2)
            pl.when(before)(lambda: signal(ready.at[1], up))

        to_right.start()
        to_left.start()

    @pl.when(last)
    def _():
        pl.semaphore_wait(barrier, 1)
        remote(
            0,
            v_ref.at[0, pl.ds(rows - HALO, HALO), :],
            edge_ref.at[pl.ds(0, HALO), :],
            {"gx": 0},
        ).start()
        signal(ready.at[1], {"gx": 0})
        signal(barrier, down)

    load.start()
    distance = jnp.abs(iota((rows, rows), 0) - iota((rows, rows), 1))
    across = [powers(c, distance) for c in COUPLINGS]
    distance = jnp.abs(iota((cols, cols), 0) - iota((cols, cols), 1))
    along = [powers(c, distance) for c in COUPLINGS]
    edge = HALO + 8
    place = iota((edge, cols), 0)
    tail = iota((HALO, cols), 0)
    above = []
    for k, c in enumerate(COUPLINGS):
        _, scale = green(c)
        near, far, side = DIFFERENCES[k]
        sum_weight = 0.0
        row_weight = 0.0
        for shift, factor in ((1, far), (0, near + far), (-1, side * (near + far)), (-2, side * far)):
            at = place - shift
            held = jnp.where((at >= 2) & (at <= HALO), powers(c, jnp.abs(HALO - at)), 0.0) / scale
            sum_weight += factor * held
            row_weight += jnp.where(at == HALO + 1, factor, 0.0)
        weight_ref[k, pl.ds(0, edge), :] = sum_weight
        weight_ref[k, pl.ds(edge + 2 * HALO, edge), :] = row_weight
        weight_ref[k, pl.ds(edge, HALO), :] = powers(c, tail)
        weight_ref[k, pl.ds(edge + HALO, HALO), :] = powers(c, jnp.abs(tail - 1))
        above.append(
            (
                jnp.where((place >= 7) & (place < edge - 2), powers(c, jnp.abs(place - 7)), 0.0) / scale,
                powers(c, HALO - 1 - tail),
                powers(c, jnp.abs(HALO - 2 - tail)),
            )
        )
    lane = iota((rows, 128), 1)
    source = iota((128, 128), 0)
    target = iota((128, 128), 1)
    sides = [[powers(c, jnp.abs(target - source + shift)) for c in COUPLINGS] for shift in (64, -64)]

    load.wait()
    u = u_ref[...]
    edge_ref[pl.ds(HALO, 8), :] = u[:8]
    near = [pltpu.roll(u[:, :128], 64, 1), pltpu.roll(u[:, cols - 128 :], 64, 1)]

    row = iota((rows, cols), 0)
    col = iota((rows, cols), 1)
    inner = (row >= 2) & (row < rows - 2)
    for out, g, s in zip((dx_ref, dxx_ref), across, stencils(u, 0)):
        out[0] = dot(g, jnp.where(inner, s, 0.0))
    inner = (col >= 2) & (col < cols - 2)
    fy = [dot(jnp.where(inner, s, 0.0), g) for g, s in zip(along, stencils(u, 1))]

    @pl.when(last)
    def _():
        pl.semaphore_wait(ready.at[0], 1)
        to_down.start()
        pl.semaphore_wait(ready.at[1], 1)
        to_right.start()
        to_left.start()

    @pl.when(first)
    def _():
        pl.semaphore_wait(ready.at[1], 1)
        remote(1, u_ref.at[pl.ds(0, HALO), :], xr, down).start()

    take(rows + HALO, recv.at[1])
    lower = stencils(jnp.where(lane < 64, pltpu.roll(yl[...], 64, 1), near[0]), 1)
    upper = stencils(jnp.where(lane < 64, near[1], pltpu.roll(yr[...], 64, 1)), 1)
    for k, out in enumerate((dy_ref, dyy_ref)):
        low = jnp.where((lane >= 2) & (lane < 66), lower[k], 0.0)
        high = jnp.where((lane >= 62) & (lane < 126), upper[k], 0.0)
        out[0] = fy[k] + jnp.concatenate(
            [dot(low, sides[0][k]), dot(high, sides[1][k])], axis=1
        )

    upper = stencils(jnp.concatenate([u[rows - 8 :], xr[...]], axis=0), 0)
    for k, out in enumerate((dx_ref, dxx_ref)):
        weight, far, close = above[k]
        total = jnp.sum(weight * upper[k], axis=0, keepdims=True)
        out[0, pl.ds(rows - HALO, HALO), :] += far * total + close * upper[k][6:7]

    take(rows + 2 * HALO, send)
    to_up.wait_recv()


def finish(
    dx_in, dy_in, dxx_in, dyy_in, edge_ref, weight_ref, dx_ref, dy_ref, dxx_ref, dyy_ref, low, pool, sem
):
    rest = pl.ds(HALO, dx_in.shape[1] - HALO)
    half = pl.ds(0, dx_in.shape[1] // 2)
    other = pl.ds(dx_in.shape[1] // 2, dx_in.shape[1] // 2)
    for part, out, place in (
        (dy_in, dy_ref, half),
        (dyy_in, dyy_ref, half),
        (dx_in, dx_ref, rest),
        (dxx_in, dxx_ref, rest),
        (dy_in, dy_ref, other),
        (dyy_in, dyy_ref, other),
    ):
        pltpu.make_async_copy(part.at[0, place, :], out.at[0, place, :], sem).start()
    edge = HALO + 8
    head = pl.ds(0, HALO)
    held = edge_ref[...]
    steps = pltpu.roll(held, edge - 1, 0) - held
    for k, (part, out) in enumerate(((dx_in, dx_ref), (dxx_in, dxx_ref))):
        total = jnp.sum(weight_ref[k, pl.ds(0, edge), :] * steps, axis=0, keepdims=True)
        source = jnp.sum(
            weight_ref[k, pl.ds(edge + 3 * HALO - 8, 16), :] * steps[HALO - 8 : HALO + 8],
            axis=0,
            keepdims=True,
        )
        low[k] = (
            part[0, head, :]
            + weight_ref[k, pl.ds(edge, HALO), :] * total
            + weight_ref[k, pl.ds(edge + HALO, HALO), :] * source
        )
        pltpu.make_async_copy(low.at[k], out.at[0, head, :], sem).start()
    pltpu.make_async_copy(pool, pool, sem).wait()


def local(nx, ny, velocity):
    _, rows, cols = velocity.shape
    out = jax.ShapeDtypeStruct(velocity.shape, F32)
    vmem = pl.BlockSpec(memory_space=pltpu.VMEM)
    anywhere = pl.BlockSpec(memory_space=pl.ANY)
    fields = pl.pallas_call(
        functools.partial(kernel, nx, ny),
        out_shape=(pltpu.VMEM(velocity.shape, F32),) * 4
        + (pltpu.VMEM((HALO + 8, cols), F32), pltpu.VMEM((2, 4 * HALO + 16, cols), F32)),
        in_specs=[anywhere],
        out_specs=[vmem] * 6,
        scratch_shapes=[
            pltpu.VMEM((rows, cols), F32),
            pltpu.VMEM((HALO, cols), F32),
            pltpu.VMEM((rows, 128), F32),
            pltpu.VMEM((rows, 128), F32),
            pltpu.VMEM((rows + 2 * HALO, cols), F32),
            pltpu.SemaphoreType.DMA((2,)),
            pltpu.SemaphoreType.REGULAR((2,)),
        ],
        compiler_params=pltpu.CompilerParams(collective_id=0, has_side_effects=True),
    )(velocity)
    return pl.pallas_call(
        finish,
        out_shape=(out,) * 4,
        in_specs=[vmem] * 6,
        out_specs=[anywhere] * 4,
        scratch_shapes=[
            pltpu.VMEM((2, HALO, cols), F32),
            pltpu.VMEM((4 * rows, cols), F32),
            pltpu.SemaphoreType.DMA,
        ],
    )(*[pltpu.with_memory_space_constraint(f, pltpu.VMEM) for f in fields])


def solution(mesh):
    placed = P(None, "gx", "gy")
    return jax.shard_map(
        functools.partial(local, mesh.shape["gx"], mesh.shape["gy"]),
        mesh=mesh,
        in_specs=(placed,),
        out_specs=(placed,) * 4,
        check_vma=False,
    )
```
